32 devices in a mesh: gx: 4 (over y, core), gy: 2 (over x), af: 4 (over z).
Axes of the slice: x: 2, y: 2, z: 4, core: 2. Of those that a mesh axis runs over, the one named last changes fastest.
Arguments:
- volume: bfloat16 [32, 16, 32, 128], P('af', 'gx', 'gy'), may hold values from -6 to 6
- weight_one: bfloat16 [32, 32, 3, 3, 3], P('af'), may hold values from -0.21875 to 0.21875
- bias_one: float32 [32], P('af'), may hold values from -1 to 1
- weight_two: bfloat16 [32, 32, 3, 3, 3], P('af'), may hold values from -0.21875 to 0.21875
- cotangent: bfloat16 [32, 16, 32, 128], P('af', 'gx', 'gy'), may hold values from -6 to 6
Outputs:
- output: bfloat16 [32, 16, 32, 128], P('af', 'gx', 'gy')
- input_grad: bfloat16 [32, 16, 32, 128], P('af', 'gx', 'gy')
- grad_one: float32 [32, 32, 3, 3, 3], P('af')
- bias_grad: float32 [32], P('af')
- grad_two: float32 [32, 32, 3, 3, 3], P('af')
The draws below stay inside these ranges and needn't reach their ends.
All inputs are finite; a program needn't handle non-finite values.
Results may differ from the reference program's by a relative error of at most 0.0065.
Values may be sent and summed in bfloat16 or wider, within the bound.
No kernel may reach another device: no remote copies, remote signals or barrier semaphores. Data moves between devices by JAX's collectives and lax.ppermute only.
A program may use at most 64 MiB of HBM per device.

```python
import jax
import jax.numpy as jnp
from jax import lax

C = 32
NZ = 128
NX = 16
NY = 32


def shard_levels(rng, extent, pieces, least, largest):
    gain = 1.0
    for dim, blocks in pieces:
        draws = jax.random.uniform(jax.random.fold_in(jax.random.fold_in(rng, 6), dim), (blocks,), jnp.float32, least / len(pieces), largest / len(pieces))
        gain = gain * jnp.repeat(jnp.exp(draws), extent[dim] // blocks).reshape((-1,) + (1,) * (len(extent) - 1 - dim))
    return gain


def scatter_about(key, dims, width, limit, cuts=(), kind=jnp.bfloat16):
    factor_of = shard_levels(key, dims, cuts, -0.22, 0.18) if cuts else 1.0
    result = jax.random.normal(key, dims, jnp.float32) * width * factor_of
    return jnp.minimum(jnp.maximum(result, -limit), limit).astype(kind)


def setup_inputs(seed: int = 0) -> dict:
    seeds = jax.random.split(jax.random.key(seed), 6)
    volume = scatter_about(seeds[0], (C, NX, NY, NZ), 1.0, 6.0, ((0, 4), (1, 4), (2, 2)))
    weight_one = scatter_about(seeds[1], (C, C, 3, 3, 3), (27 * C) ** -0.5, 0.21875, ((0, 4),))
    bias_one = jnp.clip(jax.random.uniform(seeds[2], (C,), jnp.float32, -1.0, 1.0) * shard_levels(seeds[2], (C,), ((0, 4),), -0.4, 0.0), -1.0, 1.0)
    weight_two = scatter_about(seeds[3], (C, C, 3, 3, 3), (27 * C) ** -0.5, 0.21875, ((0, 4),))
    cotangent = scatter_about(seeds[4], (C, NX, NY, NZ), 1.0, 6.0, ((0, 4), (1, 4), (2, 2)))
    return dict(volume=volume, weight_one=weight_one, bias_one=bias_one, weight_two=weight_two, cotangent=cotangent)


def conv_full(padded, weight):
    conv_out = lax.conv_general_dilated(padded[None], weight, (1, 1, 1), 'VALID', dimension_numbers=('NCDHW', 'OIDHW', 'NCDHW'), precision=lax.Precision.HIGHEST)
    return conv_out[0]

def pad_all(values):
    return jnp.pad(values, ((0, 0), (1, 1), (1, 1), (1, 1)))

def flipped(weight):
    return jnp.transpose(jnp.flip(weight, (2, 3, 4)), (1, 0, 2, 3, 4))

def kernel_grad(padded, cot_field):
    chans = cot_field.shape[0]
    size_x, size_y, size_z = (cot_field.shape[1], cot_field.shape[2], cot_field.shape[3])
    flat_cot = cot_field.reshape(chans, -1)
    blocks = []
    for off_x in range(3):
        for off_y in range(3):
            for off_z in range(3):
                window = padded[:, off_x:off_x + size_x, off_y:off_y + size_y, off_z:off_z + size_z]
                flat_win = window.reshape(padded.shape[0], -1)
                blocks.append(jnp.dot(flat_cot, flat_win.T, precision=lax.Precision.HIGHEST))
    stacked = jnp.stack(blocks, axis=-1)
    return stacked.reshape(chans, padded.shape[0], 3, 3, 3)

def reference(volume, weight_one, bias_one, weight_two, cotangent):
    first_w = weight_one.astype(jnp.float32)
    second_w = weight_two.astype(jnp.float32)
    vol_pad = pad_all(volume.astype(jnp.float32))
    pre_act = conv_full(vol_pad, first_w) + bias_one[:, None, None, None]
    hidden = jax.nn.silu(pre_act).astype(jnp.bfloat16)
    hid_pad = pad_all(hidden.astype(jnp.float32))
    output = conv_full(hid_pad, second_w).astype(jnp.bfloat16)
    cot_f = cotangent.astype(jnp.float32)
    scaling = 1.0 / jnp.sqrt(jnp.float32(NX * NY * NZ))
    grad_two = kernel_grad(hid_pad, cot_f) * scaling
    hidden_grad = conv_full(pad_all(cot_f), flipped(second_w))
    sigma_vals = jax.nn.sigmoid(pre_act)
    pre_grad = (hidden_grad * sigma_vals * (1.0 + pre_act * (1.0 - sigma_vals))).astype(jnp.bfloat16)
    pre_f = pre_grad.astype(jnp.float32)
    grad_one = kernel_grad(vol_pad, pre_f) * scaling
    bias_grad = lax.optimization_barrier(jnp.sum(pre_f, axis=(1, 2, 3))) * scaling
    input_grad = conv_full(pad_all(pre_f), flipped(first_w)).astype(jnp.bfloat16)
    return (output, input_grad, grad_one, bias_grad, grad_two)
```

```python
import functools
import math

import jax
import jax.numpy as jnp
from jax import lax
from jax.experimental import pallas as pl
from jax.experimental.pallas import tpu as pltpu
from jax.sharding import PartitionSpec as P

BF = jnp.bfloat16
F32 = jnp.float32
ALL = ("gx", "gy", "af")
RIM = 2


def place(sizes):
    me = lax.axis_index("af")
    row = lax.axis_index("gy")
    part = part_of(me, row, sizes)
    return me, row, part, row * sizes["af"] + part


def part_of(chan, row, sizes):
    return jnp.where(row % 2 == 0, chan, sizes["af"] - 1 - chan)


def own_order(parts, me):
    bit = 1
    while bit < len(parts):
        turn = (me & bit) != 0
        parts = [lax.select(turn, parts[g ^ bit], parts[g]) for g in range(len(parts))]
        bit *= 2
    return parts


def pack_body(sizes, vol_ref, cot_ref, *refs):
    groups = sizes["af"]
    outs, (flat, turned) = refs[:groups], refs[groups:]
    chans, nx, ny, nz = vol_ref.shape
    rows = ny // groups
    me, row, _, _ = place(sizes)
    for a, ref in enumerate((vol_ref, cot_ref)):
        for x in range(nx):
            flat[a, x] = ref[:, x].astype(F32).reshape(chans * ny, nz)
    for a in range(2):
        for x in range(nx):
            for y in range(ny):
                turned[y, a, x] = flat[a, x, pl.ds(y, chans, stride=ny), :].astype(BF)
    for s in range(groups):
        start = part_of(me ^ s, row, sizes) * rows
        for r in range(rows):
            outs[s][r] = turned[start + r]


def join_body(sizes, *refs):
    groups = sizes["af"]
    parts, (core_ref, first_ref, second_ref) = refs[:groups], refs[groups:]
    rows, fields, nx = parts[0].shape[:3]
    me, _, _, spot = place(sizes)
    even = spot % 2 == 0
    for a in range(fields):
        for x in range(nx):
            tiles = []
            for y in range(rows):
                cells = own_order([p[y, a, x].astype(F32) for p in parts], me)
                tiles.append(jnp.concatenate(cells, axis=0))
                core_ref[a, x, y] = tiles[-1].astype(BF)
            for h in range(RIM):
                head, tail = tiles[h], tiles[rows - RIM + h]
                first_ref[a, x, h] = lax.select(even, tail, head).astype(BF)
                second_ref[a, x, h] = lax.select(even, head, tail).astype(BF)


def y_rim(sizes, ya, yb, idx, h, spot, upper):
    even = spot % 2 == 0
    spots = sizes["gy"] * sizes["af"]
    first, second = ya[idx + (h,)].astype(F32), yb[idx + (h,)].astype(F32)
    if upper:
        got, inside = lax.select(even, first, second), spot < spots - 1
    else:
        got, inside = lax.select(even, second, first), spot > 0
    return lax.select(inside, got, jnp.zeros_like(got))


def edge_body(sizes, core, ya, yb, first_ref, second_ref):
    fields, nx, rows = core.shape[:3]
    spot = place(sizes)[3]
    even = lax.axis_index("gx") % 2 == 0
    for ref, from_tail in ((first_ref, even), (second_ref, jnp.logical_not(even))):
        start = jnp.where(from_tail, nx - RIM, 0)
        for a in range(fields):
            for h in range(RIM):
                x = start + h
                for r in range(RIM):
                    ref[a, h, r] = y_rim(sizes, ya, yb, (a, x), r, spot, False).astype(BF)
                    ref[a, h, RIM + rows + r] = y_rim(
                        sizes, ya, yb, (a, x), r, spot, True
                    ).astype(BF)
                for y in range(rows):
                    ref[a, h, RIM + y] = core[a, x, y]


def weight_pack_body(one_ref, two_ref, bias_ref, out_ref):
    taps, chans, width = one_ref.shape
    per = 128 // width
    tiles = out_ref.shape[1]
    sub = lax.broadcasted_iota(jnp.int32, (chans, width), 0)
    lane = lax.broadcasted_iota(jnp.int32, (chans, width), 1)
    bias = jnp.zeros((chans, width), F32)
    for c in range(chans):
        bias = jnp.where(sub == c, bias_ref[c], bias)
    top = bias.astype(BF).astype(F32)
    mid = (bias - top).astype(BF).astype(F32)
    low = bias - top - mid
    extra = jnp.where(lane == 0, top, jnp.where(lane == 1, mid, jnp.where(lane == 2, low, 0.0)))
    none = jnp.zeros_like(extra)
    for k, ref in enumerate((one_ref, two_ref)):
        for t in range(tiles):
            cells = []
            for j in range(per):
                tap = t * per + j
                if tap < taps:
                    cells.append(ref[tap].astype(F32))
                else:
                    cells.append(extra if k == 0 and tap == taps else none)
            out_ref[k, t] = jnp.concatenate(cells, axis=1).astype(BF)


def weight_join_body(sizes, taps, *refs):
    groups = sizes["af"]
    parts, outs = refs[:groups], refs[groups:]
    kinds, tiles, chans = parts[0].shape[:3]
    width = chans * groups
    per = 128 // width
    me = lax.axis_index("af")
    for k in range(kinds):
        plain, turned = outs[2 * k], outs[2 * k + 1]
        blocks = {}
        for t in range(tiles):
            cells = own_order([p[k, t].astype(F32) for p in parts], me)
            tile = jnp.concatenate(cells, axis=0)
            plain[:, t * 128 : (t + 1) * 128] = tile.astype(BF)
            back = tile.T
            for j in range(per):
                blocks[t * per + j] = back[j * width : (j + 1) * width]
        none = jnp.zeros((width, width), F32)
        for t in range(tiles):
            cells = []
            for j in range(per):
                tap = t * per + j
                cells.append(blocks[taps - 1 - tap] if tap < taps else none)
            turned[:, t * 128 : (t + 1) * 128] = jnp.concatenate(cells, axis=1).astype(BF)


def spread(ref, x, y, tile):
    nz = tile.shape[1]
    lane = lax.broadcasted_iota(jnp.int32, tile.shape, 1)
    below = jnp.where(lane == 0, 0.0, pltpu.roll(tile, 1, 1))
    above = jnp.where(lane == nz - 1, 0.0, pltpu.roll(tile, nz - 1, 1))
    ref[x, y] = jnp.concatenate([below, tile, above], axis=0).astype(BF)


def extra_rows(width, count):
    sub = lax.broadcasted_iota(jnp.int32, (width, count), 0)
    return jnp.where(sub < 3, 1.0, 0.0).astype(BF)


def window(ref, x, ys, extra):
    columns = []
    for y in ys:
        pieces = [ref[x + i, y + j] for i in range(3) for j in range(3)]
        columns.append(jnp.concatenate(pieces + [extra], axis=0))
    return jnp.concatenate(columns, axis=1) if len(columns) > 1 else columns[0]


def dot(left, right):
    return lax.dot_general(left, right, (((1,), (0,)), ((), ())), preferred_element_type=F32)


def dot_cells(left, right):
    return lax.dot_general(left, right, (((1,), (1,)), ((), ())), preferred_element_type=F32)


def fields_body(sizes, core, ya, yb, xa, xb, one_ref, two_ref, *refs):
    groups = sizes["af"]
    hid_ref, pre_ref = refs[:2]
    outs = refs[2 : 2 + groups]
    vol_s, cot_s, hid_s, pre_s, acc = refs[2 + groups :]
    _, nx, rows, width, nz = core.shape
    me, _, _, spot = place(sizes)
    gx = lax.axis_index("gx")
    even = gx % 2 == 0
    spots = sizes["gy"] * groups
    inside_low, inside_high = gx > 0, gx < sizes["gx"] - 1
    extra = extra_rows(width, nz)

    for a, ref in enumerate((vol_s, cot_s)):

        def middle(x, carry):
            for y in range(rows):
                spread(ref, RIM + x, RIM + y, core[a, x, y].astype(F32))
            for h in range(RIM):
                spread(ref, RIM + x, h, y_rim(sizes, ya, yb, (a, x), h, spot, False))
                spread(
                    ref, RIM + x, RIM + rows + h, y_rim(sizes, ya, yb, (a, x), h, spot, True)
                )
            return carry

        lax.fori_loop(0, nx, middle, 0)

        def sides(h, carry):
            for y in range(rows + 2 * RIM):
                first, second = xa[a, h, y].astype(F32), xb[a, h, y].astype(F32)
                none = jnp.zeros_like(first)
                low = lax.select(even, second, first)
                high = lax.select(even, first, second)
                spread(ref, h, y, lax.select(inside_low, low, none))
                spread(ref, RIM + nx + h, y, lax.select(inside_high, high, none))
            return carry

        lax.fori_loop(0, RIM, sides, 0)

    def field_row(x, carry):
        x_in = jnp.logical_and(
            jnp.logical_or(x > 0, inside_low), jnp.logical_or(x < nx + 1, inside_high)
        )
        for start in range(0, rows + 2, 2):
            ys = list(range(start, min(start + 2, rows + 2)))
            pre_act = dot(one_ref[...], window(vol_s, x, ys, extra))
            hid_grad = dot(two_ref[...], window(cot_s, x, ys, extra))
            sigma = 1.0 / (1.0 + jnp.exp(-pre_act))
            hidden = pre_act * sigma
            pre_grad = hid_grad * sigma * (1.0 + pre_act * (1.0 - sigma))
            for n, y in enumerate(ys):
                ok = x_in
                if y == 0:
                    ok = jnp.logical_and(ok, spot > 0)
                if y == rows + 1:
                    ok = jnp.logical_and(ok, spot < spots - 1)
                for full, out, stack in ((hidden, hid_ref, hid_s), (pre_grad, pre_ref, pre_s)):
                    tile = full[:, n * nz : (n + 1) * nz]
                    tile = lax.select(ok, tile, jnp.zeros_like(tile)).astype(BF)
                    out[x, y] = tile
                    spread(stack, x, y, tile.astype(F32))
        return carry

    lax.fori_loop(0, nx + 2, field_row, 0)

    acc[...] = jnp.zeros_like(acc)

    def grad_row(x, carry):
        ys = list(range(rows))
        cot = [cot_s[RIM + x, RIM + y, width : 2 * width] for y in ys]
        acc[0] += dot_cells(jnp.concatenate(cot, axis=1), window(hid_s, x, ys, extra))
        pre = [pre_s[1 + x, 1 + y, width : 2 * width] for y in ys]
        acc[1] += dot_cells(
            jnp.concatenate(pre, axis=1), window(vol_s, x + 1, [y + 1 for y in ys], extra)
        )
        return carry

    lax.fori_loop(0, nx, grad_row, 0)

    chans = width // groups
    for s in range(groups):
        start = pl.multiple_of((me ^ s) * chans, chans)
        for k in range(2):
            outs[s][k] = acc[k, pl.ds(start, chans), :]


def outputs_body(sizes, hid_ref, pre_ref, two_ref, one_ref, *refs):
    groups = sizes["af"]
    outs, (hid_s, pre_s, turned) = refs[:groups], refs[groups:]
    nx, rows, width, nz = hid_ref.shape
    nx, rows = nx - 2, rows - 2
    chans = width // groups
    me = lax.axis_index("af")
    extra = jnp.zeros((width, nz), BF)

    def fill(x, carry):
        for y in range(rows + 2):
            spread(hid_s, x, y, hid_ref[x, y].astype(F32))
            spread(pre_s, x, y, pre_ref[x, y].astype(F32))
        return carry

    lax.fori_loop(0, nx + 2, fill, 0)

    def out_row(x, carry):
        for start in range(0, rows, 2):
            ys = list(range(start, min(start + 2, rows)))
            for a, (ref, stack) in enumerate(((two_ref, hid_s), (one_ref, pre_s))):
                got = dot(ref[...], window(stack, x, ys, extra))
                for n, y in enumerate(ys):
                    for g in range(groups):
                        turned[g, y, a, x] = got[
                            g * chans : (g + 1) * chans, n * nz : (n + 1) * nz
                        ].astype(BF)
        return carry

    lax.fori_loop(0, nx, out_row, 0)
    for s in range(groups):
        outs[s][...] = turned[me ^ s]


def unpack_body(sizes, *refs):
    groups = sizes["af"]
    parts, (out_ref, grad_ref, flat) = refs[:groups], refs[groups:]
    rows, _, nx, chans, nz = parts[0].shape
    ny = rows * groups
    me, row, _, _ = place(sizes)
    for s in range(groups):
        start = part_of(me ^ s, row, sizes) * rows
        for y in range(rows):
            for a in range(2):
                for x in range(nx):
                    spot = pl.multiple_of((start + y) * chans, chans)
                    flat[a, x, pl.ds(spot, chans), :] = parts[s][y, a, x].astype(F32)
    for a, ref in enumerate((out_ref, grad_ref)):
        for x in range(nx):
            for c in range(chans):
                ref[c, x] = flat[a, x, pl.ds(c, ny, stride=chans), :].astype(BF)


def total_body(scale, taps, width, own_ref, got_ref, one_ref, two_ref, bias_ref):
    per = 128 // width
    for k, ref in ((1, one_ref), (0, two_ref)):
        total = (own_ref[k] + got_ref[k]) * scale
        for tap in range(taps):
            ref[tap] = total[:, tap * width : (tap + 1) * width]
        if k == 1:
            bias_ref[...] = total[:, taps * width : taps * width + 1]


def call(body, outs, scratch, args, specs=None, flops=0):
    moved = sum(math.prod(a.shape) * a.dtype.itemsize for a in args)
    moved += sum(math.prod(o.shape) * o.dtype.itemsize for o in outs)
    return pl.pallas_call(
        body,
        out_shape=tuple(outs),
        in_specs=specs or [pl.BlockSpec(memory_space=pltpu.VMEM)] * len(args),
        out_specs=tuple(pl.BlockSpec(memory_space=pltpu.VMEM) for _ in outs),
        scratch_shapes=scratch,
        cost_estimate=pl.CostEstimate(flops=flops, bytes_accessed=moved, transcendentals=0),
    )(*args)


def swap(value, axes, pairs):
    return lax.ppermute(value, axes, pairs)


def across(value, step, sizes):
    return swap(value, "af", [(i, i ^ step) for i in range(sizes["af"])])


def ring_pairs(count, second):
    if not second:
        return [(i, i ^ 1) for i in range(count)]
    return [(i, ((((i - 1) % count) ^ 1) + 1) % count) for i in range(count)]


def y_pairs(sizes, second):
    groups = sizes["af"]

    def spot(i):
        row, part = divmod(i, groups)
        return row * groups + (part if row % 2 == 0 else groups - 1 - part)

    pairs = ring_pairs(sizes["gy"] * groups, second)
    return [(spot(i), spot(j)) for i, j in pairs]


def body(sizes, volume, weight_one, bias_one, weight_two, cotangent):
    groups = sizes["af"]
    chans, nx, ny, nz = volume.shape
    width = chans * groups
    rows = ny // groups
    taps = 27
    tiles = -(-(taps + 1) * width // 128)
    columns = tiles * 128
    bind = functools.partial
    shape = jax.ShapeDtypeStruct

    piece = shape((rows, 2, nx, chans, nz), BF)
    sent = call(
        bind(pack_body, sizes),
        [piece] * groups,
        [pltpu.VMEM((2, nx, chans * ny, nz), F32), pltpu.VMEM((ny, 2, nx, chans, nz), BF)],
        (volume, cotangent),
    )
    parts = [sent[0]] + [across(sent[s], s, sizes) for s in range(1, groups)]

    rim = shape((2, nx, RIM, width, nz), BF)
    core, first, second = call(
        bind(join_body, sizes), [shape((2, nx, rows, width, nz), BF), rim, rim], [], parts
    )
    ya = swap(first, ("gy", "af"), y_pairs(sizes, False))
    yb = swap(second, ("gy", "af"), y_pairs(sizes, True))

    taps_first = [jnp.transpose(w, (2, 3, 4, 0, 1)).reshape(taps, chans, width) for w in (weight_one, weight_two)]
    vmem = pl.BlockSpec(memory_space=pltpu.VMEM)
    (own_w,) = call(
        weight_pack_body,
        [shape((2, tiles, chans, 128), BF)],
        [],
        (*taps_first, bias_one),
        [vmem, vmem, pl.BlockSpec(memory_space=pltpu.SMEM)],
    )

    side = shape((2, RIM, rows + 2 * RIM, width, nz), BF)
    first, second = call(bind(edge_body, sizes), [side, side], [], (core, ya, yb))
    xa = swap(first, "gx", ring_pairs(sizes["gx"], False))
    xb = swap(second, "gx", ring_pairs(sizes["gx"], True))

    weights = [own_w] + [across(own_w, s, sizes) for s in range(1, groups)]
    flat_w = shape((width, columns), BF)
    one, one_t, two, two_t = call(
        bind(weight_join_body, sizes, taps), [flat_w] * 4, [], weights
    )

    field = shape((nx + 2, rows + 2, width, nz), BF)
    share = shape((2, chans, columns), F32)
    got = call(
        bind(fields_body, sizes),
        [field, field] + [share] * groups,
        [
            pltpu.VMEM((nx + 4, rows + 4, 3 * width, nz), BF),
            pltpu.VMEM((nx + 4, rows + 4, 3 * width, nz), BF),
            pltpu.VMEM((nx + 2, rows + 2, 3 * width, nz), BF),
            pltpu.VMEM((nx + 2, rows + 2, 3 * width, nz), BF),
            pltpu.VMEM((2, width, columns), F32),
        ],
        (core, ya, yb, xa, xb, one, two_t),
        flops=4 * width * columns * nz * ((nx + 2) * (rows + 2) + nx * rows),
    )
    hidden, pre_grad, shares = got[0], got[1], got[2:]

    total = shares[0]
    for s in range(1, groups):
        total = total + across(shares[s], s, sizes)
    steps = []
    for axis in ("gy", "gx"):
        bit = 1
        while bit < sizes[axis]:
            steps.append((axis, [(i, i ^ bit) for i in range(sizes[axis])]))
            bit *= 2
    for axis, pairs in steps[:-1]:
        total = total + swap(total, axis, pairs)
    last = swap(total, *steps[-1])

    pieces = call(
        bind(outputs_body, sizes),
        [piece] * groups,
        [
            pltpu.VMEM((nx + 2, rows + 2, 3 * width, nz), BF),
            pltpu.VMEM((nx + 2, rows + 2, 3 * width, nz), BF),
            pltpu.VMEM((groups, rows, 2, nx, chans, nz), BF),
        ],
        (hidden, pre_grad, two, one_t),
        flops=4 * width * columns * nz * nx * rows,
    )
    pieces = [pieces[0]] + [across(pieces[s], s, sizes) for s in range(1, groups)]
    block = shape((chans, nx, ny, nz), BF)
    output, input_grad = call(
        bind(unpack_body, sizes),
        [block, block],
        [pltpu.VMEM((2, nx, chans * ny, nz), F32)],
        pieces,
    )

    cells = nx * sizes["gx"] * ny * sizes["gy"] * nz
    tap_grad = shape((taps, chans, width), F32)
    grad_one, grad_two, bias_grad = call(
        bind(total_body, 1.0 / math.sqrt(cells), taps, width),
        [tap_grad, tap_grad, shape((chans, 1), F32)],
        [],
        (total, last),
    )

    def unturn(grad):
        return jnp.transpose(grad.reshape(3, 3, 3, chans, width), (3, 4, 0, 1, 2))

    return output, input_grad, unturn(grad_one), bias_grad.reshape(chans), unturn(grad_two)


def solution(mesh):
    return jax.shard_map(
        functools.partial(body, dict(mesh.shape)),
        mesh=mesh,
        in_specs=(
            P("af", "gx", "gy", None),
            P("af", None, None, None, None),
            P("af"),
            P("af", None, None, None, None),
            P("af", "gx", "gy", None),
        ),
        out_specs=(
            P("af", "gx", "gy", None),
            P("af", "gx", "gy", None),
            P("af", None, None, None, None),
            P("af"),
            P("af", None, None, None, None),
        ),
        check_vma=False,
    )
```

```python
import functools
import math

import jax
import jax.numpy as jnp
from jax import lax
from jax.experimental import pallas as pl
from jax.experimental.pallas import tpu as pltpu
from jax.sharding import PartitionSpec as P


BF = jnp.bfloat16
F32 = jnp.float32
LIMIT = 20 << 20
RIM = 2


def place(sizes):
    me = lax.axis_index("af")
    row = lax.axis_index("gy")
    part = part_of(me, row, sizes)
    return me, row, part, row * sizes["af"] + part


def part_of(chan, row, sizes):
    return jnp.where(row % 2 == 0, chan, sizes["af"] - 1 - chan)


def own_order(parts, me):
    bit = 1
    while bit < len(parts):
        turn = (me & bit) != 0
        parts = [lax.select(turn, parts[g ^ bit], parts[g]) for g in range(len(parts))]
        bit *= 2
    return parts


def pack_body(sizes, vol_hbm, cot_hbm, one_hbm, two_hbm, bias_hbm, *refs):
    groups = sizes["af"]
    outs = refs[:groups]
    vol_ref, cot_ref, one_ref, two_ref, bias_ref, flat, turned, packed, sems = refs[groups:]
    chans, nx, ny, nz = vol_ref.shape
    rows = ny // groups
    me, row, _, _ = place(sizes)
    pairs = (
        (one_hbm, one_ref),
        (two_hbm, two_ref),
        (bias_hbm, bias_ref),
        (vol_hbm, vol_ref),
        (cot_hbm, cot_ref),
    )
    copies = [pltpu.make_async_copy(src, dst, sems.at[n]) for n, (src, dst) in enumerate(pairs)]
    for copy in copies:
        copy.start()
    for copy in copies[:3]:
        copy.wait()
    pack_weights(one_ref, two_ref, bias_ref, packed)
    core = lax.axis_index("gx") % 2
    cells = rows * 2 * nx
    for a, ref in enumerate((vol_ref, cot_ref)):
        copies[3 + a].wait()
        for x in range(nx):
            flat[a, x] = ref[:, x].astype(F32).reshape(chans * ny, nz)
        for x in range(nx):
            for y in range(ny):
                turned[y, a, x] = flat[a, x, pl.ds(y, chans, stride=ny), :].astype(BF)
    for s in range(groups):
        start = part_of(me ^ s, row, sizes) * rows
        for r in range(rows):
            for a in range(2):
                for x in range(nx):
                    outs[s][(r * 2 + a) * nx + x] = turned[start + r, a, x]
        outs[s][cells:] = packed[core]


def rim_starts(even, size):
    first = jnp.where(even, RIM + size, 0)
    return first, RIM + size - first


def rim_source(even, size):
    first = jnp.where(even, size - RIM, 0)
    return first, size - RIM - first


def clear_wrap(ref, spot, spots):
    @pl.when(jnp.logical_or(spot == 0, spot == spots - 1))
    def _():
        ref[...] = jnp.zeros_like(ref)


def join_body(sizes, parts_shape, *refs):
    groups = sizes["af"]
    rows, fields, nx = parts_shape
    parts, (core_ref, y_one, y_two, x_one, x_two, weight_ref) = refs[:groups], refs[groups:]
    me, _, _, spot = place(sizes)
    gx = lax.axis_index("gx")

    def whole(n):
        cells = own_order([p[n].astype(F32) for p in parts], me)
        return jnp.concatenate(cells, axis=0).astype(BF)

    for a in range(fields):
        for x in range(nx):
            for y in range(rows):
                core_ref[a, x, y] = whole((y * fields + a) * nx + x)
    for ref, start in zip((y_one, y_two), rim_source(spot % 2 == 0, rows)):
        for a in range(fields):
            for x in range(nx):
                for h in range(RIM):
                    ref[a, x, h] = core_ref[a, x, start + h]
    for ref, start in zip((x_one, x_two), rim_source(gx % 2 == 0, nx)):
        for a in range(fields):
            for h in range(RIM):
                for y in range(rows):
                    ref[a, h, y] = core_ref[a, start + h, y]
    clear_wrap(y_two, spot, sizes["gy"] * groups)
    clear_wrap(x_two, gx, sizes["gx"])
    for t in range(weight_ref.shape[1] // 128):
        weight_ref[:, t * 128 : (t + 1) * 128] = whole(rows * fields * nx + t)


def edge_body(sizes, ya, yb, first_ref, second_ref):
    fields, nx = ya.shape[:2]
    spot = place(sizes)[3]
    gx = lax.axis_index("gx")
    y_first, y_second = rim_starts(spot % 2 == 0, 0)
    for ref, start in zip((first_ref, second_ref), rim_source(gx % 2 == 0, nx)):
        for a in range(fields):
            for h in range(RIM):
                for r in range(RIM):
                    ref[a, h, y_first + r] = ya[a, start + h, r]
                    ref[a, h, y_second + r] = yb[a, start + h, r]
    clear_wrap(second_ref, gx, sizes["gx"])


def pack_weights(one_ref, two_ref, bias_ref, out_ref):
    taps, chans, width = one_ref.shape
    per = 128 // width
    tiles = out_ref.shape[1]
    sub = lax.broadcasted_iota(jnp.int32, (chans, width), 0)
    lane = lax.broadcasted_iota(jnp.int32, (chans, width), 1)
    spread_bias = jnp.broadcast_to(bias_ref[...], (chans, chans))
    diagonal = sub[:, :chans] == lane[:, :chans]
    bias = jnp.sum(jnp.where(diagonal, spread_bias, 0.0), axis=1, keepdims=True)
    bias = jnp.broadcast_to(bias, (chans, width))
    top = bias.astype(BF).astype(F32)
    mid = (bias - top).astype(BF).astype(F32)
    low = bias - top - mid
    extra = jnp.where(lane == 0, top, jnp.where(lane == 1, mid, jnp.where(lane == 2, low, 0.0)))
    none = jnp.zeros_like(extra)
    for k, ref in enumerate((one_ref, two_ref)):
        for t in range(tiles):
            cells = []
            for j in range(per):
                tap = t * per + j
                if tap < taps:
                    cells.append(ref[tap].astype(F32))
                else:
                    cells.append(extra if k == 0 and tap == taps else none)
            out_ref[k, t] = jnp.concatenate(cells, axis=1).astype(BF)


def weight_join_body(taps, mine_ref, other_ref, *outs):
    width = mine_ref.shape[0]
    tiles = mine_ref.shape[1] // 128
    per = 128 // width
    first_core = lax.axis_index("gx") % 2 == 0
    for k in range(2):
        plain, turned = outs[2 * k], outs[2 * k + 1]
        blocks = {}
        for t in range(tiles):
            at = slice(t * 128, (t + 1) * 128)
            mine, other = mine_ref[:, at].astype(F32), other_ref[:, at].astype(F32)
            tile = lax.select(first_core, (mine, other)[k], (other, mine)[k])
            plain[:, at] = tile.astype(BF)
            back = tile.T
            for j in range(per):
                blocks[t * per + j] = back[j * width : (j + 1) * width]
        none = jnp.zeros((width, width), F32)
        for t in range(tiles):
            cells = []
            for j in range(per):
                tap = t * per + j
                cells.append(blocks[taps - 1 - tap] if tap < taps else none)
            turned[:, t * 128 : (t + 1) * 128] = jnp.concatenate(cells, axis=1).astype(BF)


def spread(ref, x, y, tile):
    width, nz = tile.shape
    lane = lax.broadcasted_iota(jnp.int32, tile.shape, 1)
    none = jnp.zeros_like(tile)
    ref[x, y, :width] = jnp.where(lane == 0, none, pltpu.roll(tile, 1, 1))
    ref[x, y, width : 2 * width] = tile
    ref[x, y, 2 * width :] = jnp.where(lane == nz - 1, none, pltpu.roll(tile, nz - 1, 1))


def extra_rows(width, count):
    sub = lax.broadcasted_iota(jnp.int32, (width, count), 0)
    return jnp.where(sub < 3, 1.0, 0.0).astype(BF)


def window(get, x, ys, extra):
    columns = []
    for y in ys:
        pieces = [get(x + i, y + j) for i in range(3) for j in range(3)]
        columns.append(jnp.concatenate(pieces + [extra], axis=0))
    return jnp.concatenate(columns, axis=1) if len(columns) > 1 else columns[0]


def outside(x, size, low):
    return x < low or x >= low + size


def stacked(early, late, sizes_xy, low):
    def get(x, y, rows=slice(None)):
        nx, ny = sizes_xy
        if outside(x, nx, low) and outside(y, ny, low):
            return late[x if x < low else x - nx, y if y < low else y - ny, rows]
        return early[x, y, rows]

    return get


def dot(left, right):
    return lax.dot_general(left, right, (((1,), (0,)), ((), ())), preferred_element_type=F32)


def dot_cells(left, right):
    return lax.dot_general(left, right, (((1,), (1,)), ((), ())), preferred_element_type=F32)


def layer(sizes, shape, get_vol, get_cot, one_ref, two_ref, put_hid, put_pre, x, ys, extra):
    nx, rows, nz = shape
    spot = place(sizes)[3]
    gx = lax.axis_index("gx")
    pre_acts = dot(one_ref[...], window(get_vol, x, ys, extra))
    hid_grads = dot(two_ref[...], window(get_cot, x, ys, extra))
    for n, y in enumerate(ys):
        at = slice(n * nz, (n + 1) * nz)
        pre_act = pre_acts[:, at]
        sigma = 1.0 / (1.0 + jnp.exp(-pre_act))
        slope = sigma * (1.0 + pre_act * (1.0 - sigma))
        rules = []
        if x == 0:
            rules.append(gx > 0)
        if x == nx + 1:
            rules.append(gx < sizes["gx"] - 1)
        if y == 0:
            rules.append(spot > 0)
        if y == rows + 1:
            rules.append(spot < sizes["gy"] * sizes["af"] - 1)
        for tile, put in ((pre_act * sigma, put_hid), (hid_grads[:, at] * slope, put_pre)):
            if rules:
                ok = functools.reduce(jnp.logical_and, rules)
                tile = lax.select(ok, tile, jnp.zeros_like(tile))
            put(x, y, tile.astype(BF))


def act_body(sizes, core, ya, yb, xa, xb, one_ref, two_ref, vol_s, cot_s, hid_s, pre_s):
    _, nx, rows, width, nz = core.shape
    gx = lax.axis_index("gx")
    y_first, y_second = rim_starts(place(sizes)[3] % 2 == 0, rows)
    x_first, x_second = rim_starts(gx % 2 == 0, nx)
    extra = extra_rows(width, nz)
    for a, stack in enumerate((vol_s, cot_s)):
        for x in range(nx):
            for h in range(RIM):
                spread(stack, RIM + x, y_first + h, ya[a, x, h])
                spread(stack, RIM + x, y_second + h, yb[a, x, h])
            for y in range(rows):
                spread(stack, RIM + x, RIM + y, core[a, x, y])
        for h in range(RIM):
            for y in range(rows):
                spread(stack, x_first + h, RIM + y, xa[a, h, y])
                spread(stack, x_second + h, RIM + y, xb[a, h, y])

    def get(stack):
        return lambda x, y: stack[x, y]

    def put(stack):
        return lambda x, y, tile: spread(stack, x, y, tile)

    for x in range(nx + 2):
        for start in range(0, rows + 2, 2):
            if outside(x, nx - 2, RIM) and outside(start, rows - 2, RIM):
                continue
            layer(
                sizes, (nx, rows, nz), get(vol_s), get(cot_s), one_ref, two_ref,
                put(hid_s), put(pre_s), x, [start, start + 1], extra,
            )


def fields_body(sizes, ca, cb, one_ref, two_ref, vol_e, cot_e, hid_e, pre_e, *refs):
    hid_l, pre_l, keep_ref, send_ref, vol_l, cot_l = refs
    nx, rows = (n - 2 * RIM for n in vol_e.shape[:2])
    width, nz = ca.shape[3:]
    spot = place(sizes)[3]
    gx = lax.axis_index("gx")
    extra = extra_rows(width, nz)
    x_first, x_second = rim_starts(gx % 2 == 0, 0)
    for a, stack in enumerate((vol_l, cot_l)):
        for h in range(RIM):
            for y in range(2 * RIM):
                spread(stack, x_first + h, y, ca[a, h, y])
                spread(stack, x_second + h, y, cb[a, h, y])

    get_vol = stacked(vol_e, vol_l, (nx, rows), RIM)
    get_cot = stacked(cot_e, cot_l, (nx, rows), RIM)
    get_hid = stacked(hid_e, hid_l, (nx - 2, rows - 2), RIM)
    get_pre = stacked(pre_e, pre_l, (nx - 2, rows - 2), RIM)

    def put(stack):
        def store(x, y, tile):
            spread(stack, x if x < RIM else x - nx + 2, y if y < RIM else y - rows + 2, tile)

        return store

    for x in range(nx + 2):
        for start in range(0, rows + 2, 2):
            if outside(x, nx - 2, RIM) and outside(start, rows - 2, RIM):
                layer(
                    sizes, (nx, rows, nz), get_vol, get_cot, one_ref, two_ref,
                    put(hid_l), put(pre_l), x, [start, start + 1], extra,
                )

    middle = slice(width, 2 * width)
    acc = [None, None]
    for x in range(nx):
        ys = list(range(rows))
        cot = [get_cot(RIM + x, RIM + y, middle) for y in ys]
        pre = [get_pre(1 + x, 1 + y, middle) for y in ys]
        got = (
            dot_cells(jnp.concatenate(cot, axis=1), window(get_hid, x, ys, extra)),
            dot_cells(
                jnp.concatenate(pre, axis=1),
                window(get_vol, x + 1, [y + 1 for y in ys], extra),
            ),
        )
        acc = [g if old is None else old + g for old, g in zip(acc, got)]

    first_core = gx % 2 == 0
    keep_ref[...] = lax.select(first_core, acc[0], acc[1])
    send_ref[...] = lax.select(first_core, acc[1], acc[0])


def split_body(sizes, own_ref, got_ref, keep_ref, send_ref, total):
    groups = sizes["af"]
    me = lax.axis_index("af")
    chans = own_ref.shape[0] // groups
    for g in range(groups):
        rows = slice(g * chans, (g + 1) * chans)
        total[g] = own_ref[rows] + got_ref[rows]
    for j in range(groups // 2):
        keep_ref[j] = total[me ^ (2 * j)]
        send_ref[j] = total[me ^ (2 * j + 1)]


def halve_body(own_ref, got_ref, keep_ref, send_ref):
    for j in range(own_ref.shape[0] // 2):
        keep_ref[j] = own_ref[2 * j] + got_ref[2 * j]
        send_ref[j] = own_ref[2 * j + 1] + got_ref[2 * j + 1]


def sum_body(*refs):
    parts = [ref[...] for ref in refs[:-1]]
    while len(parts) > 1:
        parts = [parts[i] + parts[i + 1] for i in range(0, len(parts), 2)]
    refs[-1][...] = parts[0]


def outputs_body(sizes, hid_e, pre_e, hid_l, pre_l, two_ref, one_ref, *refs):
    groups = sizes["af"]
    outs, (turned,) = refs[:groups], refs[groups:]
    nx, rows = (n - 2 for n in hid_e.shape[:2])
    width, nz = two_ref.shape[0], hid_e.shape[3]
    chans = width // groups
    me = lax.axis_index("af")
    extra = jnp.zeros((width, nz), BF)
    get_hid = stacked(hid_e, hid_l, (nx - 2, rows - 2), RIM)
    get_pre = stacked(pre_e, pre_l, (nx - 2, rows - 2), RIM)
    for x in range(nx):
        for start in range(0, rows, 2):
            ys = [start, start + 1]
            for a, (ref, get) in enumerate(((two_ref, get_hid), (one_ref, get_pre))):
                got = dot(ref[...], window(get, x, ys, extra))
                for n, y in enumerate(ys):
                    for g in range(groups):
                        turned[g, y, a, x] = got[
                            g * chans : (g + 1) * chans, n * nz : (n + 1) * nz
                        ].astype(BF)
    for s in range(groups):
        outs[s][...] = turned[me ^ s]


def unpack_body(sizes, *refs):
    groups = sizes["af"]
    parts, (out_ref, grad_ref, flat) = refs[:groups], refs[groups:]
    rows, _, nx, chans, _ = parts[0].shape
    ny = rows * groups
    me, row, _, _ = place(sizes)
    for s in range(groups):
        start = part_of(me ^ s, row, sizes) * rows
        for y in range(rows):
            for a in range(2):
                for x in range(nx):
                    spot = pl.multiple_of((start + y) * chans, chans)
                    flat[a, x, pl.ds(spot, chans), :] = parts[s][y, a, x].astype(F32)
    for a, ref in enumerate((out_ref, grad_ref)):
        for x in range(nx):
            for c in range(chans):
                ref[c, x] = flat[a, x, pl.ds(c, ny, stride=chans), :].astype(BF)


def total_body(scale, taps, width, own_ref, got_ref, one_ref, two_ref, bias_ref):
    first_core = lax.axis_index("gx") % 2 == 0
    own, got = own_ref[0] * scale, got_ref[0] * scale
    chans = own.shape[0]
    two, one = lax.select(first_core, own, got), lax.select(first_core, got, own)
    for total, ref in ((one, one_ref), (two, two_ref)):
        for tap in range(taps):
            ref[tap] = total[:, tap * width : (tap + 1) * width]
    bias = jnp.broadcast_to(one[:, taps * width : taps * width + 1], (chans, chans))
    sub = lax.broadcasted_iota(jnp.int32, (chans, chans), 0)
    lane = lax.broadcasted_iota(jnp.int32, (chans, chans), 1)
    bias_ref[...] = jnp.sum(jnp.where(sub == lane, bias, 0.0), axis=0, keepdims=True)


def call(body, outs, scratch, args, specs=None, flops=0):
    moved = sum(math.prod(a.shape) * a.dtype.itemsize for a in args)
    moved += sum(math.prod(o.shape) * o.dtype.itemsize for o in outs)
    return pl.pallas_call(
        body,
        out_shape=tuple(outs),
        in_specs=specs or [pl.BlockSpec(memory_space=pltpu.VMEM)] * len(args),
        out_specs=tuple(pl.BlockSpec(memory_space=pltpu.VMEM) for _ in outs),
        scratch_shapes=scratch,
        compiler_params=pltpu.CompilerParams(vmem_limit_bytes=LIMIT),
        cost_estimate=pl.CostEstimate(flops=flops, bytes_accessed=moved, transcendentals=0),
    )(*args)


def across(value, step, sizes):
    return lax.ppermute(value, "af", [(i, i ^ step) for i in range(sizes["af"])])


def ring_pairs(count, second):
    if not second:
        return [(i, i ^ 1) for i in range(count)]
    return [(i, ((((i - 1) % count) ^ 1) + 1) % count) for i in range(count)]


def y_pairs(sizes, second):
    groups = sizes["af"]

    def spot(i):
        row, part = divmod(i, groups)
        return row * groups + (part if row % 2 == 0 else groups - 1 - part)

    pairs = ring_pairs(sizes["gy"] * groups, second)
    return [(spot(i), spot(j)) for i, j in pairs]


def body(sizes, volume, weight_one, bias_one, weight_two, cotangent):
    groups = sizes["af"]
    chans, nx, ny, nz = volume.shape
    width = chans * groups
    rows = ny // groups
    taps = 27
    tiles = -(-(taps + 1) * width // 128)
    columns = tiles * 128
    bind = functools.partial
    shape = jax.ShapeDtypeStruct
    far = range(groups - 1, 0, -1)

    cores = ring_pairs(sizes["gx"], False)

    def exchange(pieces):
        got = {s: across(pieces[s], s, sizes) for s in far}
        return [pieces[0]] + [got[s] for s in range(1, groups)]

    piece = shape((rows, 2, nx, chans, nz), BF)
    in_taps = [
        jnp.transpose(w, (2, 3, 4, 0, 1)).reshape(taps, chans, width)
        for w in (weight_one, weight_two)
    ]
    args = (volume, cotangent, *in_taps, bias_one.reshape(1, chans))
    parcel = shape((rows * 2 * nx + tiles, chans, 128), BF)
    sent = call(
        bind(pack_body, sizes),
        [parcel] * groups,
        [
            pltpu.VMEM((chans, nx, ny, nz), BF),
            pltpu.VMEM((chans, nx, ny, nz), BF),
            pltpu.VMEM((taps, chans, width), BF),
            pltpu.VMEM((taps, chans, width), BF),
            pltpu.VMEM((1, chans), F32),
            pltpu.VMEM((2, nx, chans * ny, nz), F32),
            pltpu.VMEM((ny, 2, nx, chans, nz), BF),
            pltpu.VMEM((2, tiles, chans, 128), BF),
            pltpu.SemaphoreType.DMA((5,)),
        ],
        tuple(pltpu.with_memory_space_constraint(v, pltpu.HBM) for v in args),
        [pl.BlockSpec(memory_space=pltpu.HBM)] * 5,
    )
    parts = exchange(sent)

    y_rim = shape((2, nx, RIM, width, nz), BF)
    x_rim = shape((2, RIM, rows, width, nz), BF)
    flat_w = shape((width, columns), BF)
    core, y_one, y_two, x_one, x_two, mine = call(
        bind(join_body, sizes, (rows, 2, nx)),
        [shape((2, nx, rows, width, nz), BF), y_rim, y_rim, x_rim, x_rim, flat_w],
        [],
        parts,
    )
    near, wrap = ring_pairs(sizes["gx"], False), ring_pairs(sizes["gx"], True)
    y_rims = (
        lax.ppermute(y_one, ("gy", "af"), y_pairs(sizes, False)),
        lax.ppermute(y_two, ("gy", "af"), y_pairs(sizes, True)),
    )
    x_rims = lax.ppermute(x_one, "gx", near), lax.ppermute(x_two, "gx", wrap)
    other = lax.ppermute(mine, "gx", cores)

    corner = shape((2, RIM, 2 * RIM, width, nz), BF)
    c_one, c_two = call(bind(edge_body, sizes), [corner] * 2, [], y_rims)
    corners = lax.ppermute(c_one, "gx", near), lax.ppermute(c_two, "gx", wrap)
    one, one_t, two, two_t = call(
        bind(weight_join_body, taps), [flat_w] * 4, [], (mine, other)
    )

    stack = shape((nx + 2 * RIM, rows + 2 * RIM, 3 * width, nz), BF)
    field = shape((nx + 2, rows + 2, 3 * width, nz), BF)
    late = shape((2 * RIM, 2 * RIM, 3 * width, nz), BF)
    share = shape((width, columns), F32)
    stacks = call(
        bind(act_body, sizes),
        [stack, stack, field, field],
        [],
        (core, *y_rims, *x_rims, one, two_t),
        flops=2 * width * columns * nz * (nx + 2) * (rows + 2),
    )
    hid_l, pre_l, keep, send = call(
        bind(fields_body, sizes),
        [late, late, share, share],
        [pltpu.VMEM(late.shape, BF), pltpu.VMEM(late.shape, BF)],
        (*corners, one, two_t, *stacks),
        flops=2 * width * columns * nz * ((nx + 2) * (rows + 2) + 2 * nx * rows),
    )

    half = shape((groups // 2, chans, columns), F32)
    got = lax.ppermute(send, "gx", cores)
    keep, send = call(
        bind(split_body, sizes),
        [half, half],
        [pltpu.VMEM((groups, chans, columns), F32)],
        (keep, got),
    )
    bit = 1
    while bit < groups:
        got = across(send, bit, sizes)
        if 2 * bit < groups:
            half = shape((groups // (4 * bit), chans, columns), F32)
            keep, send = call(halve_body, [half, half], [], (keep, got))
        bit *= 2

    pieces = call(
        bind(outputs_body, sizes),
        [piece] * groups,
        [pltpu.VMEM((groups, rows, 2, nx, chans, nz), BF)],
        (*stacks[2:], hid_l, pre_l, two, one_t),
        flops=4 * width * columns * nz * nx * rows,
    )

    own = shape((1, chans, columns), F32)
    (total,) = call(sum_body, [own], [], (keep, got))
    bits = []
    for axis, low in (("gx", 2), ("gy", 1)):
        while low < sizes[axis]:
            bits.append((low if axis == "gy" else low * sizes["gy"]))
            low *= 2
    while bits:
        steps = [0]
        for bit in bits[:2]:
            steps += [step ^ bit for step in steps]
        bits = bits[2:]
        count = sizes["gx"] * sizes["gy"]
        got = [
            lax.ppermute(total, ("gx", "gy"), [(i, i ^ step) for i in range(count)])
            for step in steps[1:]
        ]
        (total,) = call(sum_body, [own], [], [total, *got])
    last = lax.ppermute(total, "gx", cores)

    pieces = exchange(pieces)
    block = shape((chans, nx, ny, nz), BF)
    output, input_grad = call(
        bind(unpack_body, sizes),
        [block, block],
        [pltpu.VMEM((2, nx, chans * ny, nz), F32)],
        pieces,
    )

    cells = nx * sizes["gx"] * ny * sizes["gy"] * nz
    tap_grad = shape((taps, chans, width), F32)
    grad_one, grad_two, bias_grad = call(
        bind(total_body, 1.0 / math.sqrt(cells), taps, width),
        [tap_grad, tap_grad, shape((1, chans), F32)],
        [],
        (total, last),
    )

    def unturn(grad):
        return jnp.transpose(grad.reshape(3, 3, 3, chans, width), (3, 4, 0, 1, 2))

    return output, input_grad, unturn(grad_one), bias_grad.reshape(chans), unturn(grad_two)


def solution(mesh):
    def run(*args):
        return body(dict(mesh.shape), *args)

    return jax.shard_map(
        run,
        mesh=mesh,
        in_specs=(
            P("af", "gx", "gy", None),
            P("af", None, None, None, None),
            P("af"),
            P("af", None, None, None, None),
            P("af", "gx", "gy", None),
        ),
        out_specs=(
            P("af", "gx", "gy", None),
            P("af", "gx", "gy", None),
            P("af", None, None, None, None),
            P("af"),
            P("af", None, None, None, None),
        ),
        check_vma=False,
    )
```

```python
import functools
import math

import jax
import jax.numpy as jnp
from jax import lax
from jax.experimental import pallas as pl
from jax.experimental.pallas import tpu as pltpu
from jax.sharding import PartitionSpec as P


BF = jnp.bfloat16
F32 = jnp.float32
LIMIT = 20 << 20
RIM = 2


def place(sizes):
    me = lax.axis_index("af")
    row = lax.axis_index("gy")
    part = part_of(me, row, sizes)
    return me, row, part, row * sizes["af"] + part


def part_of(chan, row, sizes):
    return jnp.where(row % 2 == 0, chan, sizes["af"] - 1 - chan)


def own_order(parts, me):
    bit = 1
    while bit < len(parts):
        turn = (me & bit) != 0
        parts = [lax.select(turn, parts[g ^ bit], parts[g]) for g in range(len(parts))]
        bit *= 2
    return parts


def pack_body(sizes, vol_hbm, cot_hbm, one_hbm, two_hbm, bias_hbm, *refs):
    groups = sizes["af"]
    outs = refs[:groups]
    vol_ref, cot_ref, one_ref, two_ref, bias_ref, flat, turned, packed, sems = refs[groups:]
    chans, nx, ny, nz = vol_ref.shape
    rows = ny // groups
    me, row, _, _ = place(sizes)
    pairs = (
        (one_hbm, one_ref),
        (two_hbm, two_ref),
        (bias_hbm, bias_ref),
        (vol_hbm, vol_ref),
        (cot_hbm, cot_ref),
    )
    copies = [pltpu.make_async_copy(src, dst, sems.at[n]) for n, (src, dst) in enumerate(pairs)]
    for copy in copies:
        copy.start()
    for copy in copies[:3]:
        copy.wait()
    pack_weights(one_ref, two_ref, bias_ref, packed)
    core = lax.axis_index("gx") % 2
    cells = rows * 2 * nx
    for a, ref in enumerate((vol_ref, cot_ref)):
        copies[3 + a].wait()
        for x in range(nx):
            flat[a, x] = ref[:, x].astype(F32).reshape(chans * ny, nz)
        for x in range(nx):
            for y in range(ny):
                turned[y, a, x] = flat[a, x, pl.ds(y, chans, stride=ny), :].astype(BF)
    for s in range(groups):
        start = part_of(me ^ s, row, sizes) * rows
        for r in range(rows):
            for a in range(2):
                for x in range(nx):
                    outs[s][(r * 2 + a) * nx + x] = turned[start + r, a, x]
        outs[s][cells:] = packed[core]


def rim_starts(even, size):
    first = jnp.where(even, RIM + size, 0)
    return first, RIM + size - first


def rim_source(even, size):
    first = jnp.where(even, size - RIM, 0)
    return first, size - RIM - first


def clear_wrap(ref, spot, spots):
    @pl.when(jnp.logical_or(spot == 0, spot == spots - 1))
    def _():
        ref[...] = jnp.zeros_like(ref)


def join_body(sizes, parts_shape, *refs):
    groups = sizes["af"]
    rows, fields, nx = parts_shape
    parts, (core_ref, y_one, y_two, x_one, x_two, weight_ref) = refs[:groups], refs[groups:]
    me, _, _, spot = place(sizes)
    gx = lax.axis_index("gx")

    def whole(n):
        cells = own_order([p[n].astype(F32) for p in parts], me)
        return jnp.concatenate(cells, axis=0).astype(BF)

    for a in range(fields):
        for x in range(nx):
            for y in range(rows):
                core_ref[a, x, y] = whole((y * fields + a) * nx + x)
    for ref, start in zip((y_one, y_two), rim_source(spot % 2 == 0, rows)):
        for a in range(fields):
            for x in range(nx):
                for h in range(RIM):
                    ref[a, x, h] = core_ref[a, x, start + h]
    for ref, start in zip((x_one, x_two), rim_source(gx % 2 == 0, nx)):
        for a in range(fields):
            for h in range(RIM):
                for y in range(rows):
                    ref[a, h, y] = core_ref[a, start + h, y]
    clear_wrap(y_two, spot, sizes["gy"] * groups)
    clear_wrap(x_two, gx, sizes["gx"])
    for t in range(weight_ref.shape[1] // 128):
        weight_ref[:, t * 128 : (t + 1) * 128] = whole(rows * fields * nx + t)


def edge_body(sizes, ya, yb, first_ref, second_ref):
    fields, nx = ya.shape[:2]
    spot = place(sizes)[3]
    gx = lax.axis_index("gx")
    y_first, y_second = rim_starts(spot % 2 == 0, 0)
    for ref, start in zip((first_ref, second_ref), rim_source(gx % 2 == 0, nx)):
        for a in range(fields):
            for h in range(RIM):
                for r in range(RIM):
                    ref[a, h, y_first + r] = ya[a, start + h, r]
                    ref[a, h, y_second + r] = yb[a, start + h, r]
    clear_wrap(second_ref, gx, sizes["gx"])


def pack_weights(one_ref, two_ref, bias_ref, out_ref):
    taps, chans, width = one_ref.shape
    per = 128 // width
    tiles = out_ref.shape[1]
    sub = lax.broadcasted_iota(jnp.int32, (chans, width), 0)
    lane = lax.broadcasted_iota(jnp.int32, (chans, width), 1)
    spread_bias = jnp.broadcast_to(bias_ref[...], (chans, chans))
    diagonal = sub[:, :chans] == lane[:, :chans]
    bias = jnp.sum(jnp.where(diagonal, spread_bias, 0.0), axis=1, keepdims=True)
    bias = jnp.broadcast_to(bias, (chans, width))
    top = bias.astype(BF).astype(F32)
    mid = (bias - top).astype(BF).astype(F32)
    low = bias - top - mid
    extra = jnp.where(lane == 0, top, jnp.where(lane == 1, mid, jnp.where(lane == 2, low, 0.0)))
    none = jnp.zeros_like(extra)
    for k, ref in enumerate((one_ref, two_ref)):
        for t in range(tiles):
            cells = []
            for j in range(per):
                tap = t * per + j
                if tap < taps:
                    cells.append(ref[tap].astype(F32))
                else:
                    cells.append(extra if k == 0 and tap == taps else none)
            out_ref[k, t] = jnp.concatenate(cells, axis=1).astype(BF)


def weight_join_body(taps, mine_ref, other_ref, *outs):
    width = mine_ref.shape[0]
    tiles = mine_ref.shape[1] // 128
    per = 128 // width
    first_core = lax.axis_index("gx") % 2 == 0
    for k in range(2):
        plain, turned = outs[2 * k], outs[2 * k + 1]
        blocks = {}
        for t in range(tiles):
            at = slice(t * 128, (t + 1) * 128)
            mine, other = mine_ref[:, at].astype(F32), other_ref[:, at].astype(F32)
            tile = lax.select(first_core, (mine, other)[k], (other, mine)[k])
            plain[:, at] = tile.astype(BF)
            back = tile.T
            for j in range(per):
                blocks[t * per + j] = back[j * width : (j + 1) * width]
        none = jnp.zeros((width, width), F32)
        for t in range(tiles):
            cells = []
            for j in range(per):
                tap = t * per + j
                cells.append(blocks[taps - 1 - tap] if tap < taps else none)
            turned[:, t * 128 : (t + 1) * 128] = jnp.concatenate(cells, axis=1).astype(BF)


def spread(ref, x, y, tile):
    width, nz = tile.shape
    lane = lax.broadcasted_iota(jnp.int32, tile.shape, 1)
    none = jnp.zeros_like(tile)
    ref[x, y, :width] = jnp.where(lane == 0, none, pltpu.roll(tile, 1, 1))
    ref[x, y, width : 2 * width] = tile
    ref[x, y, 2 * width :] = jnp.where(lane == nz - 1, none, pltpu.roll(tile, nz - 1, 1))


def extra_rows(width, count):
    sub = lax.broadcasted_iota(jnp.int32, (width, count), 0)
    return jnp.where(sub < 3, 1.0, 0.0).astype(BF)


def window(get, x, ys, extra):
    columns = []
    for y in ys:
        pieces = [get(x + i, y + j) for i in range(3) for j in range(3)]
        columns.append(jnp.concatenate(pieces + [extra], axis=0))
    return jnp.concatenate(columns, axis=1) if len(columns) > 1 else columns[0]


def outside(x, size, low):
    return x < low or x >= low + size


def stacked(early, late, sizes_xy, low):
    def get(x, y, rows=slice(None)):
        nx, ny = sizes_xy
        if outside(x, nx, low) and outside(y, ny, low):
            return late[x if x < low else x - nx, y if y < low else y - ny, rows]
        return early[x, y, rows]

    return get


def dot(left, right):
    return lax.dot_general(left, right, (((1,), (0,)), ((), ())), preferred_element_type=F32)


def dot_cells(left, right):
    return lax.dot_general(left, right, (((1,), (1,)), ((), ())), preferred_element_type=F32)


def activate(sizes, shape, pre_acts, hid_grads, put_hid, put_pre, x, ys):
    nx, rows = shape
    spot = place(sizes)[3]
    gx = lax.axis_index("gx")
    for pre_act, hid_grad, y in zip(pre_acts, hid_grads, ys):
        sigma = 1.0 / (1.0 + jnp.exp(-pre_act))
        slope = sigma * (1.0 + pre_act * (1.0 - sigma))
        rules = []
        if x == 0:
            rules.append(gx > 0)
        if x == nx + 1:
            rules.append(gx < sizes["gx"] - 1)
        if y == 0:
            rules.append(spot > 0)
        if y == rows + 1:
            rules.append(spot < sizes["gy"] * sizes["af"] - 1)
        for tile, put in ((pre_act * sigma, put_hid), (hid_grad * slope, put_pre)):
            if rules:
                ok = functools.reduce(jnp.logical_and, rules)
                tile = lax.select(ok, tile, jnp.zeros_like(tile))
            put(x, y, tile.astype(BF))


def apart(value, count):
    size = value.shape[1] // count
    return [value[:, n * size : (n + 1) * size] for n in range(count)]


def row_pairs(nx, rows):
    for x in range(nx + 2):
        for start in range(0, rows + 2, 2):
            late = outside(x, nx - 2, RIM) and outside(start, rows - 2, RIM)
            yield x, [start, start + 1], late


def corner_place(x, size):
    return x if x < RIM else x - size


def act_body(sizes, core, ya, yb, xa, xb, one_ref, two_ref, vol_s, cot_s, hid_s, pre_s, *rest):
    _, nx, rows, width, nz = core.shape
    gx = lax.axis_index("gx")
    y_first, y_second = rim_starts(place(sizes)[3] % 2 == 0, rows)
    x_first, x_second = rim_starts(gx % 2 == 0, nx)
    extra = extra_rows(width, nz)
    none = jnp.zeros((3 * width, nz), BF)
    for a, stack in enumerate((vol_s, cot_s)):
        for x in range(nx):
            for h in range(RIM):
                spread(stack, RIM + x, y_first + h, ya[a, x, h])
                spread(stack, RIM + x, y_second + h, yb[a, x, h])
            for y in range(rows):
                spread(stack, RIM + x, RIM + y, core[a, x, y])
        for h in range(RIM):
            for y in range(rows):
                spread(stack, x_first + h, RIM + y, xa[a, h, y])
                spread(stack, x_second + h, RIM + y, xb[a, h, y])

    def get(stack):
        def load(x, y):
            return none if outside(x, nx, RIM) and outside(y, rows, RIM) else stack[x, y]

        return load

    def put(stack):
        return lambda x, y, tile: spread(stack, x, y, tile)

    for later in (False, True):
        for x, ys, late in row_pairs(nx, rows):
            if late != later:
                continue
            sums = [
                apart(dot(ref[...], window(get(stack), x, ys, extra)), len(ys))
                for ref, stack in ((one_ref, vol_s), (two_ref, cot_s))
            ]
            if not late:
                activate(sizes, (nx, rows), *sums, put(hid_s), put(pre_s), x, ys)
                continue
            for tiles, ref in zip(sums, rest):
                for y, tile in zip(ys, tiles):
                    ref[corner_place(x, nx - 2), corner_place(y, rows - 2)] = tile


def tap_grad_of(get, center, nx, rows, extra):
    acc = [None] * 3
    for x in range(nx + 2):
        near = [i for i in range(3) if 0 <= x - i < nx]
        for start in range(0, rows, 2):
            ys = [start, start + 1]
            columns = [
                jnp.concatenate([get(x, y + j) for j in range(3)] + [extra], axis=0) for y in ys
            ]
            left = [
                jnp.concatenate([center(x - i, y) for y in ys], axis=1) for i in near
            ]
            got = dot_cells(jnp.concatenate(left, axis=0), jnp.concatenate(columns, axis=1))
            size = got.shape[0] // len(near)
            for n, i in enumerate(near):
                part = got[n * size : (n + 1) * size]
                acc[i] = part if acc[i] is None else acc[i] + part
    width = acc[0].shape[0]
    return jnp.concatenate(
        [part[:, : 9 * width] for part in acc] + [acc[0][:, 9 * width :]], axis=1
    )


def fields_body(sizes, ca, cb, one_ref, two_ref, vol_e, cot_e, hid_e, pre_e, *refs):
    vol_p, cot_p, hid_l, pre_l, keep_ref, send_ref, vol_l, cot_l = refs
    nx, rows = (n - 2 * RIM for n in vol_e.shape[:2])
    width, nz = ca.shape[3:]
    gx = lax.axis_index("gx")
    extra = extra_rows(width, nz)
    none = jnp.zeros((3 * width, nz), BF)
    x_first, x_second = rim_starts(gx % 2 == 0, 0)
    for a, stack in enumerate((vol_l, cot_l)):
        for h in range(RIM):
            for y in range(2 * RIM):
                spread(stack, x_first + h, y, ca[a, h, y])
                spread(stack, x_second + h, y, cb[a, h, y])

    get_vol = stacked(vol_e, vol_l, (nx, rows), RIM)
    get_cot = stacked(cot_e, cot_l, (nx, rows), RIM)
    get_hid = stacked(hid_e, hid_l, (nx - 2, rows - 2), RIM)
    get_pre = stacked(pre_e, pre_l, (nx - 2, rows - 2), RIM)

    def put(stack):
        def store(x, y, tile):
            spread(stack, corner_place(x, nx - 2), corner_place(y, rows - 2), tile)

        return store

    for x, ys, late in row_pairs(nx, rows):
        if not late:
            continue
        far = [i for i in range(3) if outside(x + i, nx, RIM)]
        js = [j for j in range(3) if any(outside(y + j, rows, RIM) for y in ys)]
        sums = []
        for ref, known, get in ((one_ref, vol_p, get_vol), (two_ref, cot_p, get_cot)):
            left = []
            for i in far:
                begin = (3 * i + js[0]) * 3 * width
                left.append(ref[:, begin : begin + len(js) * 3 * width])
            columns = []
            for y in ys:
                pieces = [
                    get(x + i, y + j) if outside(y + j, rows, RIM) else none
                    for i in far
                    for j in js
                ]
                columns.append(jnp.concatenate(pieces, axis=0))
            got = dot(jnp.concatenate(left, axis=1), jnp.concatenate(columns, axis=1))
            place_x = corner_place(x, nx - 2)
            sums.append(
                [
                    known[place_x, corner_place(y, rows - 2)] + tile
                    for y, tile in zip(ys, apart(got, len(ys)))
                ]
            )
        activate(sizes, (nx, rows), *sums, put(hid_l), put(pre_l), x, ys)

    middle = slice(width, 2 * width)
    two = tap_grad_of(
        get_hid, lambda x, y: get_cot(RIM + x, RIM + y, middle), nx, rows, extra
    )
    one = tap_grad_of(
        lambda x, y: get_vol(x + 1, y + 1),
        lambda x, y: get_pre(1 + x, 1 + y, middle),
        nx,
        rows,
        extra,
    )
    first_core = gx % 2 == 0
    keep_ref[...] = lax.select(first_core, two, one)
    send_ref[...] = lax.select(first_core, one, two)


def split_body(sizes, own_ref, got_ref, keep_ref, send_ref, total):
    groups = sizes["af"]
    me = lax.axis_index("af")
    chans = own_ref.shape[0] // groups
    for g in range(groups):
        rows = slice(g * chans, (g + 1) * chans)
        total[g] = own_ref[rows] + got_ref[rows]
    for j in range(groups // 2):
        keep_ref[j] = total[me ^ (2 * j)]
        send_ref[j] = total[me ^ (2 * j + 1)]


def halve_body(own_ref, got_ref, keep_ref, send_ref):
    for j in range(own_ref.shape[0] // 2):
        keep_ref[j] = own_ref[2 * j] + got_ref[2 * j]
        send_ref[j] = own_ref[2 * j + 1] + got_ref[2 * j + 1]


def sum_body(*refs):
    parts = [ref[...] for ref in refs[:-1]]
    while len(parts) > 1:
        parts = [parts[i] + parts[i + 1] for i in range(0, len(parts), 2)]
    refs[-1][...] = parts[0]


def outputs_body(sizes, hid_e, pre_e, hid_l, pre_l, two_ref, one_ref, *refs):
    groups = sizes["af"]
    outs, (turned,) = refs[:groups], refs[groups:]
    nx, rows = (n - 2 for n in hid_e.shape[:2])
    width, nz = two_ref.shape[0], hid_e.shape[3]
    chans = width // groups
    me = lax.axis_index("af")
    extra = jnp.zeros((width, nz), BF)
    get_hid = stacked(hid_e, hid_l, (nx - 2, rows - 2), RIM)
    get_pre = stacked(pre_e, pre_l, (nx - 2, rows - 2), RIM)
    for x in range(nx):
        for start in range(0, rows, 2):
            ys = [start, start + 1]
            for a, (ref, get) in enumerate(((two_ref, get_hid), (one_ref, get_pre))):
                got = dot(ref[...], window(get, x, ys, extra))
                for n, y in enumerate(ys):
                    for g in range(groups):
                        turned[g, y, a, x] = got[
                            g * chans : (g + 1) * chans, n * nz : (n + 1) * nz
                        ].astype(BF)
    for s in range(groups):
        outs[s][...] = turned[me ^ s]


def finish_body(sizes, scale, taps, width, *refs):
    groups = sizes["af"]
    parts, totals = refs[:groups], refs[groups : groups + 4]
    out_ref, grad_ref, one_ref, two_ref, bias_ref, flat = refs[groups + 4 :]
    total_body(scale, taps, width, *totals, one_ref, two_ref, bias_ref)
    rows, _, nx, chans, _ = parts[0].shape
    ny = rows * groups
    me, row, _, _ = place(sizes)
    for s in range(groups):
        start = part_of(me ^ s, row, sizes) * rows
        for y in range(rows):
            for a in range(2):
                for x in range(nx):
                    spot = pl.multiple_of((start + y) * chans, chans)
                    flat[a, x, pl.ds(spot, chans), :] = parts[s][y, a, x].astype(F32)
    for a, ref in enumerate((out_ref, grad_ref)):
        for x in range(nx):
            for c in range(chans):
                ref[c, x] = flat[a, x, pl.ds(c, ny, stride=chans), :].astype(BF)


def total_body(scale, taps, width, own, near, cross, core, one_ref, two_ref, bias_ref):
    first_core = lax.axis_index("gx") % 2 == 0
    own, got = (own[0] + near[0]) * scale, (core[0] + cross[0]) * scale
    chans = own.shape[0]
    two, one = lax.select(first_core, own, got), lax.select(first_core, got, own)
    for total, ref in ((one, one_ref), (two, two_ref)):
        for tap in range(taps):
            ref[tap] = total[:, tap * width : (tap + 1) * width]
    bias = jnp.broadcast_to(one[:, taps * width : taps * width + 1], (chans, chans))
    sub = lax.broadcasted_iota(jnp.int32, (chans, chans), 0)
    lane = lax.broadcasted_iota(jnp.int32, (chans, chans), 1)
    bias_ref[...] = jnp.sum(jnp.where(sub == lane, bias, 0.0), axis=0, keepdims=True)


def call(body, outs, scratch, args, specs=None, flops=0):
    moved = sum(math.prod(a.shape) * a.dtype.itemsize for a in args)
    moved += sum(math.prod(o.shape) * o.dtype.itemsize for o in outs)
    return pl.pallas_call(
        body,
        out_shape=tuple(outs),
        in_specs=specs or [pl.BlockSpec(memory_space=pltpu.VMEM)] * len(args),
        out_specs=tuple(pl.BlockSpec(memory_space=pltpu.VMEM) for _ in outs),
        scratch_shapes=scratch,
        compiler_params=pltpu.CompilerParams(vmem_limit_bytes=LIMIT),
        cost_estimate=pl.CostEstimate(flops=flops, bytes_accessed=moved, transcendentals=0),
    )(*args)


def across(value, step, sizes):
    return lax.ppermute(value, "af", [(i, i ^ step) for i in range(sizes["af"])])


def ring_pairs(count, second):
    if not second:
        return [(i, i ^ 1) for i in range(count)]
    return [(i, ((((i - 1) % count) ^ 1) + 1) % count) for i in range(count)]


def y_pairs(sizes, second):
    groups = sizes["af"]

    def spot(i):
        row, part = divmod(i, groups)
        return row * groups + (part if row % 2 == 0 else groups - 1 - part)

    pairs = ring_pairs(sizes["gy"] * groups, second)
    return [(spot(i), spot(j)) for i, j in pairs]


def body(sizes, volume, weight_one, bias_one, weight_two, cotangent):
    groups = sizes["af"]
    chans, nx, ny, nz = volume.shape
    width = chans * groups
    rows = ny // groups
    taps = 27
    tiles = -(-(taps + 1) * width // 128)
    columns = tiles * 128
    bind = functools.partial
    shape = jax.ShapeDtypeStruct
    far = range(groups - 1, 0, -1)

    cores = ring_pairs(sizes["gx"], False)

    def exchange(pieces):
        got = {s: across(pieces[s], s, sizes) for s in far}
        return [pieces[0]] + [got[s] for s in range(1, groups)]

    piece = shape((rows, 2, nx, chans, nz), BF)
    in_taps = [
        jnp.transpose(w, (2, 3, 4, 0, 1)).reshape(taps, chans, width)
        for w in (weight_one, weight_two)
    ]
    args = (volume, cotangent, *in_taps, bias_one.reshape(1, chans))
    parcel = shape((rows * 2 * nx + tiles, chans, 128), BF)
    sent = call(
        bind(pack_body, sizes),
        [parcel] * groups,
        [
            pltpu.VMEM((chans, nx, ny, nz), BF),
            pltpu.VMEM((chans, nx, ny, nz), BF),
            pltpu.VMEM((taps, chans, width), BF),
            pltpu.VMEM((taps, chans, width), BF),
            pltpu.VMEM((1, chans), F32),
            pltpu.VMEM((2, nx, chans * ny, nz), F32),
            pltpu.VMEM((ny, 2, nx, chans, nz), BF),
            pltpu.VMEM((2, tiles, chans, 128), BF),
            pltpu.SemaphoreType.DMA((5,)),
        ],
        tuple(pltpu.with_memory_space_constraint(v, pltpu.HBM) for v in args),
        [pl.BlockSpec(memory_space=pltpu.HBM)] * 5,
    )
    parts = exchange(sent)

    y_rim = shape((2, nx, RIM, width, nz), BF)
    x_rim = shape((2, RIM, rows, width, nz), BF)
    flat_w = shape((width, columns), BF)
    core, y_one, y_two, x_one, x_two, mine = call(
        bind(join_body, sizes, (rows, 2, nx)),
        [shape((2, nx, rows, width, nz), BF), y_rim, y_rim, x_rim, x_rim, flat_w],
        [],
        parts,
    )
    near, wrap = ring_pairs(sizes["gx"], False), ring_pairs(sizes["gx"], True)
    y_rims = (
        lax.ppermute(y_one, ("gy", "af"), y_pairs(sizes, False)),
        lax.ppermute(y_two, ("gy", "af"), y_pairs(sizes, True)),
    )
    x_rims = lax.ppermute(x_one, "gx", near), lax.ppermute(x_two, "gx", wrap)
    other = lax.ppermute(mine, "gx", cores)

    corner = shape((2, RIM, 2 * RIM, width, nz), BF)
    c_one, c_two = call(bind(edge_body, sizes), [corner] * 2, [], y_rims)
    corners = lax.ppermute(c_one, "gx", near), lax.ppermute(c_two, "gx", wrap)
    one, one_t, two, two_t = call(
        bind(weight_join_body, taps), [flat_w] * 4, [], (mine, other)
    )

    stack = shape((nx + 2 * RIM, rows + 2 * RIM, 3 * width, nz), BF)
    field = shape((nx + 2, rows + 2, 3 * width, nz), BF)
    late = shape((2 * RIM, 2 * RIM, 3 * width, nz), BF)
    known = shape((2 * RIM, 2 * RIM, width, nz), F32)
    share = shape((width, columns), F32)
    stacks = call(
        bind(act_body, sizes),
        [stack, stack, field, field, known, known],
        [],
        (core, *y_rims, *x_rims, one, two_t),
        flops=2 * width * columns * nz * (nx + 2) * (rows + 2),
    )
    hid_l, pre_l, keep, send = call(
        bind(fields_body, sizes),
        [late, late, share, share],
        [pltpu.VMEM(late.shape, BF), pltpu.VMEM(late.shape, BF)],
        (*corners, one, two_t, *stacks),
        flops=2 * width * columns * nz * ((nx + 2) * (rows + 2) + 2 * nx * rows),
    )

    half = shape((groups // 2, chans, columns), F32)
    got = lax.ppermute(send, "gx", cores)
    keep, send = call(
        bind(split_body, sizes),
        [half, half],
        [pltpu.VMEM((groups, chans, columns), F32)],
        (keep, got),
    )
    bit = 1
    while bit < groups:
        got = across(send, bit, sizes)
        if 2 * bit < groups:
            half = shape((groups // (4 * bit), chans, columns), F32)
            keep, send = call(halve_body, [half, half], [], (keep, got))
        bit *= 2

    pieces = call(
        bind(outputs_body, sizes),
        [piece] * groups,
        [pltpu.VMEM((groups, rows, 2, nx, chans, nz), BF)],
        (*stacks[2:4], hid_l, pre_l, two, one_t),
        flops=4 * width * columns * nz * nx * rows,
    )

    own = shape((1, chans, columns), F32)
    (total,) = call(sum_body, [own], [], (keep, got))
    count = sizes["gx"] * sizes["gy"]
    bits = [1 << n for n in range((count - 1).bit_length())]
    bits.remove(sizes["gy"])
    bits.reverse()
    for bit in bits[:-1]:
        got = lax.ppermute(total, ("gx", "gy"), [(i, i ^ bit) for i in range(count)])
        (total,) = call(sum_body, [own], [], (total, got))
    got = [
        lax.ppermute(total, ("gx", "gy"), [(i, i ^ step) for i in range(count)])
        for step in (bits[-1], bits[-1] ^ sizes["gy"], sizes["gy"])
    ]

    pieces = exchange(pieces)
    block = shape((chans, nx, ny, nz), BF)
    cells = nx * sizes["gx"] * ny * sizes["gy"] * nz
    tap_grad = shape((taps, chans, width), F32)
    output, input_grad, grad_one, grad_two, bias_grad = call(
        bind(finish_body, sizes, 1.0 / math.sqrt(cells), taps, width),
        [block, block, tap_grad, tap_grad, shape((1, chans), F32)],
        [pltpu.VMEM((2, nx, chans * ny, nz), F32)],
        (*pieces, total, *got),
    )

    def unturn(grad):
        return jnp.transpose(grad.reshape(3, 3, 3, chans, width), (3, 4, 0, 1, 2))

    return output, input_grad, unturn(grad_one), bias_grad.reshape(chans), unturn(grad_two)


def solution(mesh):
    def run(*args):
        return body(dict(mesh.shape), *args)

    return jax.shard_map(
        run,
        mesh=mesh,
        in_specs=(
            P("af", "gx", "gy", None),
            P("af", None, None, None, None),
            P("af"),
            P("af", None, None, None, None),
            P("af", "gx", "gy", None),
        ),
        out_specs=(
            P("af", "gx", "gy", None),
            P("af", "gx", "gy", None),
            P("af", None, None, None, None),
            P("af"),
            P("af", None, None, None, None),
        ),
        check_vma=False,
    )
```

```python
import functools
import math

import jax
import jax.numpy as jnp
from jax import lax
from jax.experimental import pallas as pl
from jax.experimental.pallas import tpu as pltpu
from jax.sharding import PartitionSpec as P


BF = jnp.bfloat16
F32 = jnp.float32
ALL = ("gx", "gy", "af")
LIMIT = 20 << 20
RIM = 2


def place(sizes):
    me = lax.axis_index("af")
    row = lax.axis_index("gy")
    part = part_of(me, row, sizes)
    return me, row, part, row * sizes["af"] + part


def part_of(chan, row, sizes):
    return jnp.where(row % 2 == 0, chan, sizes["af"] - 1 - chan)


def own_order(parts, me):
    bit = 1
    while bit < len(parts):
        turn = (me & bit) != 0
        parts = [lax.select(turn, parts[g ^ bit], parts[g]) for g in range(len(parts))]
        bit *= 2
    return parts


def pack_body(sizes, vol_hbm, cot_hbm, one_hbm, two_hbm, bias_hbm, *refs):
    groups = sizes["af"]
    outs = refs[:groups]
    vol_ref, cot_ref, one_ref, two_ref, bias_ref, flat, turned, packed, sems = refs[groups:]
    chans, nx, ny, nz = vol_ref.shape
    rows = ny // groups
    me, row, _, _ = place(sizes)
    pairs = (
        (one_hbm, one_ref),
        (two_hbm, two_ref),
        (bias_hbm, bias_ref),
        (vol_hbm, vol_ref),
        (cot_hbm, cot_ref),
    )
    copies = [pltpu.make_async_copy(src, dst, sems.at[n]) for n, (src, dst) in enumerate(pairs)]
    for copy in copies:
        copy.start()
    for copy in copies[:3]:
        copy.wait()
    pack_weights(one_ref, two_ref, bias_ref, packed)
    core = lax.axis_index("gx") % 2
    cells = rows * 2 * nx
    for a, ref in enumerate((vol_ref, cot_ref)):
        copies[3 + a].wait()
        for x in range(nx):
            flat[a, x] = ref[:, x].astype(F32).reshape(chans * ny, nz)
        for x in range(nx):
            for y in range(ny):
                turned[y, a, x] = flat[a, x, pl.ds(y, chans, stride=ny), :].astype(BF)
    for s in range(groups):
        start = part_of(me ^ s, row, sizes) * rows
        for r in range(rows):
            for a in range(2):
                for x in range(nx):
                    outs[s][(r * 2 + a) * nx + x] = turned[start + r, a, x]
        outs[s][cells:] = packed[core]


def rim_starts(even, size):
    first = jnp.where(even, RIM + size, 0)
    return first, RIM + size - first


def rim_source(even, size):
    first = jnp.where(even, size - RIM, 0)
    return first, size - RIM - first


def clear_wrap(ref, spot, spots):
    @pl.when(jnp.logical_or(spot == 0, spot == spots - 1))
    def _():
        ref[...] = jnp.zeros_like(ref)


def join_body(sizes, parts_shape, *refs):
    groups = sizes["af"]
    rows, fields, nx = parts_shape
    parts, (core_ref, y_one, y_two, x_one, x_two, weight_ref) = refs[:groups], refs[groups:]
    me, _, _, spot = place(sizes)
    gx = lax.axis_index("gx")

    def whole(n):
        cells = own_order([p[n].astype(F32) for p in parts], me)
        return jnp.concatenate(cells, axis=0).astype(BF)

    for a in range(fields):
        for x in range(nx):
            for y in range(rows):
                core_ref[a, x, y] = whole((y * fields + a) * nx + x)
    for ref, start in zip((y_one, y_two), rim_source(spot % 2 == 0, rows)):
        for a in range(fields):
            for x in range(nx):
                for h in range(RIM):
                    ref[a, x, h] = core_ref[a, x, start + h]
    for ref, start in zip((x_one, x_two), rim_source(gx % 2 == 0, nx)):
        for a in range(fields):
            for h in range(RIM):
                for y in range(rows):
                    ref[a, h, y] = core_ref[a, start + h, y]
    clear_wrap(y_two, spot, sizes["gy"] * groups)
    clear_wrap(x_two, gx, sizes["gx"])
    for t in range(weight_ref.shape[1] // 128):
        weight_ref[:, t * 128 : (t + 1) * 128] = whole(rows * fields * nx + t)


def edge_body(sizes, ya, yb, first_ref, second_ref):
    fields, nx = ya.shape[:2]
    spot = place(sizes)[3]
    gx = lax.axis_index("gx")
    y_first, y_second = rim_starts(spot % 2 == 0, 0)
    for ref, start in zip((first_ref, second_ref), rim_source(gx % 2 == 0, nx)):
        for a in range(fields):
            for h in range(RIM):
                for r in range(RIM):
                    ref[a, h, y_first + r] = ya[a, start + h, r]
                    ref[a, h, y_second + r] = yb[a, start + h, r]
    clear_wrap(second_ref, gx, sizes["gx"])


def pack_weights(one_ref, two_ref, bias_ref, out_ref):
    taps, chans, width = one_ref.shape
    per = 128 // width
    tiles = out_ref.shape[1]
    sub = lax.broadcasted_iota(jnp.int32, (chans, width), 0)
    lane = lax.broadcasted_iota(jnp.int32, (chans, width), 1)
    spread_bias = jnp.broadcast_to(bias_ref[...], (chans, chans))
    diagonal = sub[:, :chans] == lane[:, :chans]
    bias = jnp.sum(jnp.where(diagonal, spread_bias, 0.0), axis=1, keepdims=True)
    bias = jnp.broadcast_to(bias, (chans, width))
    top = bias.astype(BF).astype(F32)
    mid = (bias - top).astype(BF).astype(F32)
    low = bias - top - mid
    extra = jnp.where(lane == 0, top, jnp.where(lane == 1, mid, jnp.where(lane == 2, low, 0.0)))
    none = jnp.zeros_like(extra)
    for k, ref in enumerate((one_ref, two_ref)):
        for t in range(tiles):
            cells = []
            for j in range(per):
                tap = t * per + j
                if tap < taps:
                    cells.append(ref[tap].astype(F32))
                else:
                    cells.append(extra if k == 0 and tap == taps else none)
            out_ref[k, t] = jnp.concatenate(cells, axis=1).astype(BF)


def weight_join_body(taps, mine_ref, other_ref, *outs):
    width = mine_ref.shape[0]
    tiles = mine_ref.shape[1] // 128
    per = 128 // width
    first_core = lax.axis_index("gx") % 2 == 0
    for k in range(2):
        plain, turned = outs[2 * k], outs[2 * k + 1]
        blocks = {}
        for t in range(tiles):
            at = slice(t * 128, (t + 1) * 128)
            mine, other = mine_ref[:, at].astype(F32), other_ref[:, at].astype(F32)
            tile = lax.select(first_core, (mine, other)[k], (other, mine)[k])
            plain[:, at] = tile.astype(BF)
            back = tile.T
            for j in range(per):
                blocks[t * per + j] = back[j * width : (j + 1) * width]
        none = jnp.zeros((width, width), F32)
        for t in range(tiles):
            cells = []
            for j in range(per):
                tap = t * per + j
                cells.append(blocks[taps - 1 - tap] if tap < taps else none)
            turned[:, t * 128 : (t + 1) * 128] = jnp.concatenate(cells, axis=1).astype(BF)


def spread(ref, x, y, tile):
    width, nz = tile.shape
    lane = lax.broadcasted_iota(jnp.int32, tile.shape, 1)
    none = jnp.zeros_like(tile)
    ref[x, y, :width] = jnp.where(lane == 0, none, pltpu.roll(tile, 1, 1))
    ref[x, y, width : 2 * width] = tile
    ref[x, y, 2 * width :] = jnp.where(lane == nz - 1, none, pltpu.roll(tile, nz - 1, 1))


def extra_rows(width, count):
    sub = lax.broadcasted_iota(jnp.int32, (width, count), 0)
    return jnp.where(sub < 3, 1.0, 0.0).astype(BF)


def window(get, x, ys, extra):
    columns = []
    for y in ys:
        pieces = [get(x + i, y + j) for i in range(3) for j in range(3)]
        columns.append(jnp.concatenate(pieces + [extra], axis=0))
    return jnp.concatenate(columns, axis=1) if len(columns) > 1 else columns[0]


def outside(x, size, low):
    return x < low or x >= low + size


def stacked(early, late, sizes_xy, low):
    def get(x, y, rows=slice(None)):
        nx, ny = sizes_xy
        if outside(x, nx, low) and outside(y, ny, low):
            return late[x if x < low else x - nx, y if y < low else y - ny, rows]
        return early[x, y, rows]

    return get


def dot(left, right):
    return lax.dot_general(left, right, (((1,), (0,)), ((), ())), preferred_element_type=F32)


def dot_cells(left, right):
    return lax.dot_general(left, right, (((1,), (1,)), ((), ())), preferred_element_type=F32)


def activate(sizes, shape, pre_acts, hid_grads, put_hid, put_pre, x, ys):
    nx, rows = shape
    spot = place(sizes)[3]
    gx = lax.axis_index("gx")
    for pre_act, hid_grad, y in zip(pre_acts, hid_grads, ys):
        sigma = 1.0 / (1.0 + jnp.exp(-pre_act))
        slope = sigma * (1.0 + pre_act * (1.0 - sigma))
        rules = []
        if x == 0:
            rules.append(gx > 0)
        if x == nx + 1:
            rules.append(gx < sizes["gx"] - 1)
        if y == 0:
            rules.append(spot > 0)
        if y == rows + 1:
            rules.append(spot < sizes["gy"] * sizes["af"] - 1)
        for tile, put in ((pre_act * sigma, put_hid), (hid_grad * slope, put_pre)):
            if rules:
                ok = functools.reduce(jnp.logical_and, rules)
                tile = lax.select(ok, tile, jnp.zeros_like(tile))
            put(x, y, tile.astype(BF))


def apart(value, count):
    size = value.shape[1] // count
    return [value[:, n * size : (n + 1) * size] for n in range(count)]


def row_pairs(nx, rows):
    for x in range(nx + 2):
        for start in range(0, rows + 2, 2):
            late = outside(x, nx - 2, RIM) and outside(start, rows - 2, RIM)
            yield x, [start, start + 1], late


def corner_place(x, size):
    return x if x < RIM else x - size


def act_body(sizes, core, ya, yb, xa, xb, one_ref, two_ref, vol_s, cot_s, hid_s, pre_s, *rest):
    _, nx, rows, width, nz = core.shape
    gx = lax.axis_index("gx")
    y_first, y_second = rim_starts(place(sizes)[3] % 2 == 0, rows)
    x_first, x_second = rim_starts(gx % 2 == 0, nx)
    extra = extra_rows(width, nz)
    none = jnp.zeros((3 * width, nz), BF)
    for a, stack in enumerate((vol_s, cot_s)):
        for x in range(nx):
            for h in range(RIM):
                spread(stack, RIM + x, y_first + h, ya[a, x, h])
                spread(stack, RIM + x, y_second + h, yb[a, x, h])
            for y in range(rows):
                spread(stack, RIM + x, RIM + y, core[a, x, y])
        for h in range(RIM):
            for y in range(rows):
                spread(stack, x_first + h, RIM + y, xa[a, h, y])
                spread(stack, x_second + h, RIM + y, xb[a, h, y])

    def get(stack):
        def load(x, y):
            return none if outside(x, nx, RIM) and outside(y, rows, RIM) else stack[x, y]

        return load

    def put(stack):
        return lambda x, y, tile: spread(stack, x, y, tile)

    for later in (False, True):
        for x, ys, late in row_pairs(nx, rows):
            if late != later:
                continue
            sums = [
                apart(dot(ref[...], window(get(stack), x, ys, extra)), len(ys))
                for ref, stack in ((one_ref, vol_s), (two_ref, cot_s))
            ]
            if not late:
                activate(sizes, (nx, rows), *sums, put(hid_s), put(pre_s), x, ys)
                continue
            for tiles, ref in zip(sums, rest):
                for y, tile in zip(ys, tiles):
                    ref[corner_place(x, nx - 2), corner_place(y, rows - 2)] = tile


def tap_grad_of(get, center, nx, rows, extra):
    acc = [None] * 3
    for x in range(nx + 2):
        near = [i for i in range(3) if 0 <= x - i < nx]
        for start in range(0, rows, 2):
            ys = [start, start + 1]
            columns = [
                jnp.concatenate([get(x, y + j) for j in range(3)] + [extra], axis=0) for y in ys
            ]
            left = [
                jnp.concatenate([center(x - i, y) for y in ys], axis=1) for i in near
            ]
            got = dot_cells(jnp.concatenate(left, axis=0), jnp.concatenate(columns, axis=1))
            size = got.shape[0] // len(near)
            for n, i in enumerate(near):
                part = got[n * size : (n + 1) * size]
                acc[i] = part if acc[i] is None else acc[i] + part
    width = acc[0].shape[0]
    return jnp.concatenate(
        [part[:, : 9 * width] for part in acc] + [acc[0][:, 9 * width :]], axis=1
    )


def fields_body(sizes, ca, cb, one_ref, two_ref, vol_e, cot_e, hid_e, pre_e, *refs):
    vol_p, cot_p, hid_l, pre_l, keep_ref, send_ref, vol_l, cot_l = refs
    nx, rows = (n - 2 * RIM for n in vol_e.shape[:2])
    width, nz = ca.shape[3:]
    gx = lax.axis_index("gx")
    extra = extra_rows(width, nz)
    none = jnp.zeros((3 * width, nz), BF)
    x_first, x_second = rim_starts(gx % 2 == 0, 0)
    for a, stack in enumerate((vol_l, cot_l)):
        for h in range(RIM):
            for y in range(2 * RIM):
                spread(stack, x_first + h, y, ca[a, h, y])
                spread(stack, x_second + h, y, cb[a, h, y])

    get_vol = stacked(vol_e, vol_l, (nx, rows), RIM)
    get_cot = stacked(cot_e, cot_l, (nx, rows), RIM)
    get_hid = stacked(hid_e, hid_l, (nx - 2, rows - 2), RIM)
    get_pre = stacked(pre_e, pre_l, (nx - 2, rows - 2), RIM)

    def put(stack):
        def store(x, y, tile):
            spread(stack, corner_place(x, nx - 2), corner_place(y, rows - 2), tile)

        return store

    for x, ys, late in row_pairs(nx, rows):
        if not late:
            continue
        far = [i for i in range(3) if outside(x + i, nx, RIM)]
        js = [j for j in range(3) if any(outside(y + j, rows, RIM) for y in ys)]
        sums = []
        for ref, known, get in ((one_ref, vol_p, get_vol), (two_ref, cot_p, get_cot)):
            left = []
            for i in far:
                begin = (3 * i + js[0]) * 3 * width
                left.append(ref[:, begin : begin + len(js) * 3 * width])
            columns = []
            for y in ys:
                pieces = [
                    get(x + i, y + j) if outside(y + j, rows, RIM) else none
                    for i in far
                    for j in js
                ]
                columns.append(jnp.concatenate(pieces, axis=0))
            got = dot(jnp.concatenate(left, axis=1), jnp.concatenate(columns, axis=1))
            place_x = corner_place(x, nx - 2)
            sums.append(
                [
                    known[place_x, corner_place(y, rows - 2)] + tile
                    for y, tile in zip(ys, apart(got, len(ys)))
                ]
            )
        activate(sizes, (nx, rows), *sums, put(hid_l), put(pre_l), x, ys)

    middle = slice(width, 2 * width)
    two = tap_grad_of(
        get_hid, lambda x, y: get_cot(RIM + x, RIM + y, middle), nx, rows, extra
    )
    one = tap_grad_of(
        lambda x, y: get_vol(x + 1, y + 1),
        lambda x, y: get_pre(1 + x, 1 + y, middle),
        nx,
        rows,
        extra,
    )
    first_core = gx % 2 == 0
    keep_ref[...] = lax.select(first_core, two, one)
    send_ref[...] = lax.select(first_core, one, two)


def split_body(sizes, own_ref, got_ref, keep_ref, send_ref, total):
    groups = sizes["af"]
    me = lax.axis_index("af")
    chans = own_ref.shape[0] // groups
    for g in range(groups):
        rows = slice(g * chans, (g + 1) * chans)
        total[g] = own_ref[rows] + got_ref[rows]
    for j in range(groups // 2):
        keep_ref[j] = total[me ^ (2 * j)]
        send_ref[j] = total[me ^ (2 * j + 1)]


def halve_body(own_ref, got_ref, keep_ref, send_ref):
    for j in range(own_ref.shape[0] // 2):
        keep_ref[j] = own_ref[2 * j] + got_ref[2 * j]
        send_ref[j] = own_ref[2 * j + 1] + got_ref[2 * j + 1]


def sum_body(*refs):
    parts = [ref[...] for ref in refs[:-1]]
    while len(parts) > 1:
        parts = [parts[i] + parts[i + 1] for i in range(0, len(parts), 2)]
    refs[-1][...] = parts[0]


def outputs_body(sizes, hid_e, pre_e, hid_l, pre_l, two_ref, one_ref, *refs):
    groups = sizes["af"]
    outs, (turned,) = refs[:groups], refs[groups:]
    nx, rows = (n - 2 for n in hid_e.shape[:2])
    width, nz = two_ref.shape[0], hid_e.shape[3]
    chans = width // groups
    me = lax.axis_index("af")
    extra = jnp.zeros((width, nz), BF)
    get_hid = stacked(hid_e, hid_l, (nx - 2, rows - 2), RIM)
    get_pre = stacked(pre_e, pre_l, (nx - 2, rows - 2), RIM)
    for x in range(nx):
        for start in range(0, rows, 2):
            ys = [start, start + 1]
            for a, (ref, get) in enumerate(((two_ref, get_hid), (one_ref, get_pre))):
                got = dot(ref[...], window(get, x, ys, extra))
                for n, y in enumerate(ys):
                    for g in range(groups):
                        turned[g, y, a, x] = got[
                            g * chans : (g + 1) * chans, n * nz : (n + 1) * nz
                        ].astype(BF)
    for s in range(groups):
        outs[s][...] = turned[me ^ s]


def finish_body(sizes, scale, taps, width, *refs):
    groups = sizes["af"]
    parts, totals = refs[:groups], refs[groups : groups + 4]
    out_ref, grad_ref, one_ref, two_ref, bias_ref, flat = refs[groups + 4 :]
    total_body(scale, taps, width, *totals, one_ref, two_ref, bias_ref)
    rows, _, nx, chans, _ = parts[0].shape
    ny = rows * groups
    me, row, _, _ = place(sizes)
    for s in range(groups):
        start = part_of(me ^ s, row, sizes) * rows
        for y in range(rows):
            for a in range(2):
                for x in range(nx):
                    spot = pl.multiple_of((start + y) * chans, chans)
                    flat[a, x, pl.ds(spot, chans), :] = parts[s][y, a, x].astype(F32)
    for a, ref in enumerate((out_ref, grad_ref)):
        for x in range(nx):
            for c in range(chans):
                ref[c, x] = flat[a, x, pl.ds(c, ny, stride=chans), :].astype(BF)


def total_body(scale, taps, width, own, near, cross, core, one_ref, two_ref, bias_ref):
    first_core = lax.axis_index("gx") % 2 == 0
    own, got = (own[0] + near[0]) * scale, (core[0] + cross[0]) * scale
    chans = own.shape[0]
    two, one = lax.select(first_core, own, got), lax.select(first_core, got, own)
    for total, ref in ((one, one_ref), (two, two_ref)):
        for tap in range(taps):
            ref[tap] = total[:, tap * width : (tap + 1) * width]
    bias = jnp.broadcast_to(one[:, taps * width : taps * width + 1], (chans, chans))
    sub = lax.broadcasted_iota(jnp.int32, (chans, chans), 0)
    lane = lax.broadcasted_iota(jnp.int32, (chans, chans), 1)
    bias_ref[...] = jnp.sum(jnp.where(sub == lane, bias, 0.0), axis=0, keepdims=True)


def call(body, outs, scratch, args, specs=None, flops=0):
    moved = sum(math.prod(a.shape) * a.dtype.itemsize for a in args)
    moved += sum(math.prod(o.shape) * o.dtype.itemsize for o in outs)
    return pl.pallas_call(
        body,
        out_shape=tuple(outs),
        in_specs=specs or [pl.BlockSpec(memory_space=pltpu.VMEM)] * len(args),
        out_specs=tuple(pl.BlockSpec(memory_space=pltpu.VMEM) for _ in outs),
        scratch_shapes=scratch,
        compiler_params=pltpu.CompilerParams(vmem_limit_bytes=LIMIT),
        cost_estimate=pl.CostEstimate(flops=flops, bytes_accessed=moved, transcendentals=0),
    )(*args)


def across(value, step, sizes):
    return lax.ppermute(value, "af", [(i, i ^ step) for i in range(sizes["af"])])


def ring_pairs(count, second):
    if not second:
        return [(i, i ^ 1) for i in range(count)]
    return [(i, ((((i - 1) % count) ^ 1) + 1) % count) for i in range(count)]


def y_pairs(sizes, second):
    groups = sizes["af"]

    def spot(i):
        row, part = divmod(i, groups)
        return row * groups + (part if row % 2 == 0 else groups - 1 - part)

    pairs = ring_pairs(sizes["gy"] * groups, second)
    return [(spot(i), spot(j)) for i, j in pairs]


def body(sizes, volume, weight_one, bias_one, weight_two, cotangent):
    groups = sizes["af"]
    chans, nx, ny, nz = volume.shape
    width = chans * groups
    rows = ny // groups
    taps = 27
    tiles = -(-(taps + 1) * width // 128)
    columns = tiles * 128
    bind = functools.partial
    shape = jax.ShapeDtypeStruct
    far = range(groups - 1, 0, -1)

    cores = ring_pairs(sizes["gx"], False)

    def exchange(pieces):
        got = {s: across(pieces[s], s, sizes) for s in far}
        return [pieces[0]] + [got[s] for s in range(1, groups)]

    piece = shape((rows, 2, nx, chans, nz), BF)
    in_taps = [
        jnp.transpose(w, (2, 3, 4, 0, 1)).reshape(taps, chans, width)
        for w in (weight_one, weight_two)
    ]
    args = (volume, cotangent, *in_taps, bias_one.reshape(1, chans))
    parcel = shape((rows * 2 * nx + tiles, chans, 128), BF)
    sent = call(
        bind(pack_body, sizes),
        [parcel] * groups,
        [
            pltpu.VMEM((chans, nx, ny, nz), BF),
            pltpu.VMEM((chans, nx, ny, nz), BF),
            pltpu.VMEM((taps, chans, width), BF),
            pltpu.VMEM((taps, chans, width), BF),
            pltpu.VMEM((1, chans), F32),
            pltpu.VMEM((2, nx, chans * ny, nz), F32),
            pltpu.VMEM((ny, 2, nx, chans, nz), BF),
            pltpu.VMEM((2, tiles, chans, 128), BF),
            pltpu.SemaphoreType.DMA((5,)),
        ],
        tuple(pltpu.with_memory_space_constraint(v, pltpu.HBM) for v in args),
        [pl.BlockSpec(memory_space=pltpu.HBM)] * 5,
    )
    parts = exchange(sent)

    y_rim = shape((2, nx, RIM, width, nz), BF)
    x_rim = shape((2, RIM, rows, width, nz), BF)
    flat_w = shape((width, columns), BF)
    core, y_one, y_two, x_one, x_two, mine = call(
        bind(join_body, sizes, (rows, 2, nx)),
        [shape((2, nx, rows, width, nz), BF), y_rim, y_rim, x_rim, x_rim, flat_w],
        [],
        parts,
    )
    near, wrap = ring_pairs(sizes["gx"], False), ring_pairs(sizes["gx"], True)
    y_rims = (
        lax.ppermute(y_one, ("gy", "af"), y_pairs(sizes, False)),
        lax.ppermute(y_two, ("gy", "af"), y_pairs(sizes, True)),
    )
    x_rims = lax.ppermute(x_one, "gx", near), lax.ppermute(x_two, "gx", wrap)
    other = lax.ppermute(mine, "gx", cores)

    corner = shape((2, RIM, 2 * RIM, width, nz), BF)
    c_one, c_two = call(bind(edge_body, sizes), [corner] * 2, [], y_rims)
    corners = lax.ppermute(c_one, "gx", near), lax.ppermute(c_two, "gx", wrap)
    one, one_t, two, two_t = call(
        bind(weight_join_body, taps), [flat_w] * 4, [], (mine, other)
    )

    stack = shape((nx + 2 * RIM, rows + 2 * RIM, 3 * width, nz), BF)
    field = shape((nx + 2, rows + 2, 3 * width, nz), BF)
    late = shape((2 * RIM, 2 * RIM, 3 * width, nz), BF)
    known = shape((2 * RIM, 2 * RIM, width, nz), F32)
    share = shape((width, columns), F32)
    stacks = call(
        bind(act_body, sizes),
        [stack, stack, field, field, known, known],
        [],
        (core, *y_rims, *x_rims, one, two_t),
        flops=2 * width * columns * nz * (nx + 2) * (rows + 2),
    )
    hid_l, pre_l, keep, send = call(
        bind(fields_body, sizes),
        [late, late, share, share],
        [pltpu.VMEM(late.shape, BF), pltpu.VMEM(late.shape, BF)],
        (*corners, one, two_t, *stacks),
        flops=2 * width * columns * nz * ((nx + 2) * (rows + 2) + 2 * nx * rows),
    )

    half = shape((groups // 2, chans, columns), F32)
    got = lax.ppermute(send, "gx", cores)
    keep, send = call(
        bind(split_body, sizes),
        [half, half],
        [pltpu.VMEM((groups, chans, columns), F32)],
        (keep, got),
    )
    count = sizes["gx"] * sizes["gy"]
    bits = [1 << n for n in range((count - 1).bit_length())]
    bits.remove(sizes["gy"])
    bits.reverse()
    bit = 1
    while 2 * bit < groups:
        got = across(send, bit, sizes)
        half = shape((groups // (4 * bit), chans, columns), F32)
        keep, send = call(halve_body, [half, half], [], (keep, got))
        bit *= 2
    step = bits[0]
    held = [
        keep,
        lax.ppermute(keep, ("gx", "gy"), [(i, i ^ step) for i in range(count)]),
        across(send, bit, sizes),
        lax.ppermute(send, ALL, [(i, i ^ (step * groups) ^ bit) for i in range(count * groups)]),
    ]

    pieces = call(
        bind(outputs_body, sizes),
        [piece] * groups,
        [pltpu.VMEM((groups, rows, 2, nx, chans, nz), BF)],
        (*stacks[2:4], hid_l, pre_l, two, one_t),
        flops=4 * width * columns * nz * nx * rows,
    )

    own = shape((1, chans, columns), F32)
    (total,) = call(sum_body, [own], [], held)
    for step in bits[1:-1]:
        got = lax.ppermute(total, ("gx", "gy"), [(i, i ^ step) for i in range(count)])
        (total,) = call(sum_body, [own], [], (total, got))
    got = [
        lax.ppermute(total, ("gx", "gy"), [(i, i ^ step) for i in range(count)])
        for step in (bits[-1], bits[-1] ^ sizes["gy"], sizes["gy"])
    ]

    pieces = exchange(pieces)
    block = shape((chans, nx, ny, nz), BF)
    cells = nx * sizes["gx"] * ny * sizes["gy"] * nz
    tap_grad = shape((taps, chans, width), F32)
    output, input_grad, grad_one, grad_two, bias_grad = call(
        bind(finish_body, sizes, 1.0 / math.sqrt(cells), taps, width),
        [block, block, tap_grad, tap_grad, shape((1, chans), F32)],
        [pltpu.VMEM((2, nx, chans * ny, nz), F32)],
        (*pieces, total, *got),
    )

    def unturn(grad):
        return jnp.transpose(grad.reshape(3, 3, 3, chans, width), (3, 4, 0, 1, 2))

    return output, input_grad, unturn(grad_one), bias_grad.reshape(chans), unturn(grad_two)


def solution(mesh):
    def run(*args):
        return body(dict(mesh.shape), *args)

    return jax.shard_map(
        run,
        mesh=mesh,
        in_specs=(
            P("af", "gx", "gy", None),
            P("af", None, None, None, None),
            P("af"),
            P("af", None, None, None, None),
            P("af", "gx", "gy", None),
        ),
        out_specs=(
            P("af", "gx", "gy", None),
            P("af", "gx", "gy", None),
            P("af", None, None, None, None),
            P("af"),
            P("af", None, None, None, None),
        ),
        check_vma=False,
    )
```
